256 devices in a mesh: gx: 16 (over x, y), gy: 16 (over z, core).
Axes of the slice: x: 4, y: 4, z: 8, core: 2. Of those that a mesh axis runs over, the one named last changes fastest.
Arguments:
- adjoint: float32 [5, 64, 256, 256], P(None, 'gx', 'gy'), may hold values from -6 to 6
- jac_x: bfloat16 [5, 5, 64, 256, 256], P(None, None, 'gx', 'gy'), may hold values from -2.5 to 2.5
- jac_y: bfloat16 [5, 5, 64, 256, 256], P(None, None, 'gx', 'gy'), may hold values from -2.5 to 2.5
- alpha_x: float32 [64], replicated, may hold values from 0.49375 to 0.498125
- metric_x: float32 [64], P('gx'), may hold values from 0.15 to 0.6
- alpha_y: float32 [256], replicated, may hold values from 0.49960938 to 0.49988282
- metric_y: float32 [256], P('gy'), may hold values from 0.15 to 0.6
- surf_values: float32 [256, 5, 512], P(('gx', 'gy')), may hold values from -12 to 12
- surf_cells: int32 [256, 512], P(('gx', 'gy')), may hold values from 0 to 16383
- surf_owner: int32 [256, 512, 1], P(('gx', 'gy')), may hold values from 0 to 255; in each aligned block of 512 rows (0 to 511, 512 to 1023, ..., all dimensions but the last counted through in order) at most 4 rows name the same one
Outputs:
- adjoint_rhs: float32 [5, 64, 256, 256], P(None, 'gx', 'gy')
The draws below stay inside these ranges and needn't reach their ends.
Inputs may be any that keep to these rules, and one draw needn't show every extreme that they name: `surf_owner`: within the 512 points of one device no owner appears more than 4 times, and some owner appears exactly 4 times.
All inputs are finite; a program needn't handle non-finite values.
Results may differ from the reference program's by a relative error of at most 0.0003.
Values sent between devices are 32-bit elements; how exact they have to be, the bound alone decides.
A program may use at most 64 MiB of HBM per device.

```python
import math
import jax
import jax.numpy as jnp
import numpy as np
from jax import lax

FIELDS = 5
CX = 4
CY = 16
CZ = 256
SURF = 512
CAP = 4
NX = 64
NY = 256
NZ = 256
N_GY = 16
DEVICES = 256


def plant(values, own_key, smallest, largest):
    extent = values.shape
    place = [jax.random.randint(jax.random.fold_in(own_key, axis), (), 0, extent[axis]) for axis in range(len(extent))]
    values = values.at[tuple(place)].set(smallest)
    longest = extent.index(max(extent))
    place[longest] = (place[longest] + 1) % extent[longest]
    return values.at[tuple(place)].set(largest)


def levels(rng, dims, cuts, smallest, largest):
    def one(dim, shards_of):
        draws = jax.random.uniform(jax.random.fold_in(jax.random.fold_in(rng, 6), dim), (shards_of,), jnp.float32, smallest / len(cuts), largest / len(cuts))
        return jnp.repeat(jnp.exp(draws), dims[dim] // shards_of).reshape((-1,) + (1,) * (len(dims) - dim - 1))

    gain = one(*cuts[0])
    for cut in cuts[1:]:
        gain = gain * one(*cut)
    return gain


def deal_out(stream_key, own, number, rows, number_of, top, most, slope):
    sequence = jax.random.permutation(stream_key, number_of)
    heavy_load, common = load_shares(number_of, rows * top, most, slope, True), load_shares(number_of, rows * top, most, slope, False)
    places = jnp.arange(number_of)

    def named(sizes, turn):
        used = int((sizes > 0).sum())
        fixed = max(1, used // 4)
        moved = fixed + (places - fixed + turn * (used - fixed)) % max(1, number_of - fixed)
        return jnp.zeros((number_of,), jnp.int32).at[sequence[jnp.where(places < fixed, places, moved)]].set(jnp.asarray(sizes, jnp.int32))

    sizes = jnp.where(number % 4 == 0, named(heavy_load, number // 4), named(common, number - number // 4 - 1))
    mixed = jax.random.permutation(jax.random.fold_in(own, 3), number_of)
    donor, taker = mixed[0:number_of // 2 * 2:2], mixed[1:number_of // 2 * 2:2]
    room = jnp.minimum(sizes[donor] - 1, most - sizes[taker]) // 2
    room = jnp.where((donor == sequence[0]) | (taker == sequence[0]) | (sizes[taker] == 0), 0, jnp.maximum(room, 0))
    moved = jax.random.randint(jax.random.fold_in(own, 4), (number_of // 2,), 0, 1 << 20) % (room + 1)
    sizes = sizes.at[donor].add(-moved).at[taker].add(moved)
    labels = jnp.searchsorted(jnp.cumsum(sizes), jnp.arange(rows * top), side="right").astype(jnp.int32)
    table = labels.reshape(top, rows).T
    table = table[jax.random.permutation(jax.random.fold_in(own, 1), rows)]
    turn = jax.random.randint(jax.random.fold_in(own, 2), (rows, 1), 0, top)
    return jnp.take_along_axis(table, (jnp.arange(top)[None, :] + turn) % top, axis=1)


def load_shares(count, total, limit, slope, full):
    weights = [(1 << 20) // math.isqrt(grade ** slope) + 1 for grade in range(1, count + 1)]
    largest = limit if full else min(limit, max(-(-total // count), total * weights[0] // sum(weights)))
    least = 1 if total - largest >= count - 1 else 0
    holding, rest = [largest] + [least] * (count - 1), total - largest - least * (count - 1)
    while rest > 0:
        candidates = [i for i in range(1, count) if holding[i] < largest] or [i for i in range(1, count) if holding[i] < limit]
        mass, remaining = sum([weights[i] for i in candidates]), rest
        for i in candidates:
            extra = min(limit - holding[i], max(1, remaining * weights[i] // mass), rest)
            holding[i] = holding[i] + extra
            rest = rest - extra
    return np.array(holding)


def normal_values(rng, dims, width, most, split=(), held_as=jnp.bfloat16):
    values = jax.random.normal(rng, dims, jnp.float32) * width
    if len(split) > 0:
        values = levels(rng, dims, split, -0.22, 0.18) * values
    return jnp.clip(values, min=-most, max=most).astype(held_as)


def setup_inputs(seed: int = 0) -> dict:
    key_list = jax.random.split(jax.random.key(seed), 11)
    adjoint = normal_values(key_list[0], (FIELDS, NX, NY, NZ), 1.0, 6.0, ((1, 16), (2, 16)), jnp.float32)
    jac_x = normal_values(key_list[1], (FIELDS, FIELDS, NX, NY, NZ), FIELDS ** -0.5, 2.5, ((2, 16), (3, 16)))
    jac_y = normal_values(key_list[2], (FIELDS, FIELDS, NX, NY, NZ), FIELDS ** -0.5, 2.5, ((2, 16), (3, 16)))
    alpha_x = jnp.clip(jax.random.uniform(key_list[3], (NX,), jnp.float32, 0.49375, 0.498125), 0.49375, 0.498125)
    metric_x = jnp.clip(jnp.exp(math.log(0.6) - 1.3862944 * jax.random.uniform(key_list[4], (NX,), jnp.float32) ** levels(key_list[4], (NX,), ((0, 16),), -0.2, 0.2)), 0.15, 0.6)
    alpha_y = jnp.clip(jax.random.uniform(key_list[5], (NY,), jnp.float32, 0.49960938, 0.49988282), 0.49960938, 0.49988282)
    metric_y = jnp.clip(jnp.exp(math.log(0.6) - 1.3862944 * jax.random.uniform(key_list[6], (NY,), jnp.float32) ** levels(key_list[6], (NY,), ((0, 16),), -0.2, 0.2)), 0.15, 0.6)
    surf_values = normal_values(key_list[7], (DEVICES, FIELDS, SURF), 2.0, 12.0, ((0, 256),), jnp.float32)
    surf_cells = plant(jax.random.randint(key_list[8], (DEVICES, SURF), 0, CX * CY * CZ), jax.random.fold_in(key_list[8], 1), 0, (CX * CY * CZ) - 1).astype(jnp.int32)
    surf_owner_keys = jax.random.split(jax.random.fold_in(key_list[9], 1), DEVICES * SURF // SURF)
    surf_owner_turns = jax.random.permutation(jax.random.fold_in(key_list[9], 3), DEVICES * SURF // SURF)
    surf_owner = jax.vmap(lambda own, number: deal_out(jax.random.fold_in(key_list[9], 2), own, number, SURF, DEVICES, 1, CAP, 2))(surf_owner_keys, surf_owner_turns).reshape((DEVICES, SURF, 1))
    return dict(adjoint=adjoint, jac_x=jac_x, jac_y=jac_y, alpha_x=alpha_x, metric_x=metric_x, alpha_y=alpha_y, metric_y=metric_y, surf_values=surf_values, surf_cells=surf_cells, surf_owner=surf_owner)


def shaped(vector, line_axis):
    return vector.reshape((1,) * line_axis + (-1,) + (1,) * (3 - line_axis))


def coefficients(alpha_line):
    lower_diag = alpha_line.at[0].set(0.0)
    upper_diag = alpha_line.at[-1].set(0.0)

    def advance(carried, pieces):
        below_now, above_now = pieces
        pivot_now = 1.0 - below_now * carried
        ratio_now = above_now / pivot_now
        return ratio_now, (pivot_now, ratio_now)

    _, (pivots, ratios) = lax.scan(advance, jnp.zeros((), jnp.float32), (lower_diag, upper_diag))
    return lower_diag, pivots, ratios


def flux_of(jacobian, state_field):
    outputs = []
    for target in range(FIELDS):
        summed = jacobian[0, target].astype(jnp.float32) * state_field[0]
        for source in range(1, FIELDS):
            summed = summed + jacobian[source, target].astype(jnp.float32) * state_field[source]
        outputs.append(summed)
    return jnp.stack(outputs)


def derivative(flux_field, alpha_line, metric_line, line_axis):
    cells_line = flux_field.shape[line_axis]
    widths = [(0, 0)] * 4
    widths[line_axis] = (2, 2)
    padded = jnp.pad(flux_field, widths)
    coef_a = shaped((2.0 / 3.0) * (alpha_line + 2.0), line_axis)
    coef_b = shaped((4.0 * alpha_line - 1.0) / 3.0, line_axis)

    def window(offset):
        return lax.slice_in_dim(padded, offset, offset + cells_line, axis=line_axis)

    right_side = 0.5 * coef_a * (window(3) - window(1)) + 0.25 * coef_b * (window(4) - window(0))
    line_data = jnp.moveaxis(right_side, line_axis, 0)
    lower_diag, pivots, ratios = coefficients(alpha_line)

    def forward(carried, pieces):
        below_now, pivot_now, column = pieces
        result = (column - below_now * carried) / pivot_now
        return result, result

    _, eliminated = lax.scan(forward, jnp.zeros_like(line_data[0]), (lower_diag, pivots, line_data))

    def backward(carried, pieces):
        ratio_now, column = pieces
        result = column - ratio_now * carried
        return result, result

    _, solved = lax.scan(backward, jnp.zeros_like(line_data[0]), (ratios, eliminated), reverse=True)
    slopes = jnp.moveaxis(solved, 0, line_axis)
    return slopes * shaped(metric_line, line_axis)


def reference(adjoint, jac_x, jac_y, alpha_x, metric_x, alpha_y, metric_y, surf_values, surf_cells, surf_owner):
    deriv_x = derivative(flux_of(jac_x, adjoint), alpha_x, metric_x, 1)
    deriv_y = derivative(flux_of(jac_y, adjoint), alpha_y, metric_y, 2)
    owners = surf_owner.reshape(-1)
    cell_ids = surf_cells.reshape(-1)
    payload = jnp.moveaxis(surf_values, 1, 0).reshape(FIELDS, -1)
    grid_x = (owners // N_GY) * CX + cell_ids // (CY * CZ)
    grid_y = (owners % N_GY) * CY + (cell_ids // CZ) % CY
    grid_z = cell_ids % CZ
    forcing = jnp.zeros((FIELDS, NX, NY, NZ), jnp.float32).at[:, grid_x, grid_y, grid_z].add(payload)
    return forcing - (deriv_x + deriv_y)
```

```python
import functools

import jax
import jax.numpy as jnp
from jax import lax
from jax.experimental import pallas as pl
from jax.experimental.pallas import tpu as pltpu
from jax.sharding import PartitionSpec as P

F32 = jnp.float32
BF16 = jnp.bfloat16
MESH = pl.DeviceIdType.MESH
FIELDS = 5
CX = 4
CY = 16
CZ = 256
NGX = 16
NGY = 16
POINTS = 512
OWNERS = 8
XROWS = 40
YROWS = 32
RROWS = 24
HIGH = lax.Precision.HIGHEST


def iota(shape, dim):
    return lax.broadcasted_iota(jnp.int32, shape, dim)


def column(row, rows, lane_of):
    width = row.shape[1]
    wide = jnp.broadcast_to(row, (rows, width))
    picked = iota((rows, width), 1) == lane_of(iota((rows, width), 0))
    return jnp.sum(jnp.where(picked, wide, 0.0), axis=1, keepdims=True)


def reduce_cyclic(below, diag, above, sides, axis, distances):
    count = below.shape[axis]
    for d in distances:
        inv = 1.0 / diag
        low = -below * pltpu.roll(inv, d, axis)
        high = -above * pltpu.roll(inv, count - d, axis)
        sides = [
            s + low * pltpu.roll(s, d, axis) + high * pltpu.roll(s, count - d, axis) for s in sides
        ]
        diag = diag + low * pltpu.roll(above, d, axis) + high * pltpu.roll(below, count - d, axis)
        below = low * pltpu.roll(below, d, axis)
        above = high * pltpu.roll(above, count - d, axis)
    inv = 1.0 / diag
    return [s * inv for s in sides]


def stencil(offset, coef_a, coef_b):
    zero = jnp.zeros_like(coef_a)
    out = jnp.where(offset == 1, 0.5 * coef_a, zero)
    out = jnp.where(offset == -1, -0.5 * coef_a, out)
    out = jnp.where(offset == 2, 0.25 * coef_b, out)
    return jnp.where(offset == -2, -0.25 * coef_b, out)


def coef_of(alpha):
    return (2.0 / 3.0) * (alpha + 2.0), (4.0 * alpha - 1.0) / 3.0


def x_matrix(alpha_row):
    n = NGX * CX
    alpha = jnp.broadcast_to(column(alpha_row, n, lambda i: i), (n, 128))
    i = iota((n, 128), 0)
    c = iota((n, 128), 1)
    station = jnp.where(c < n, (c % NGX) * CX + c // NGX, -100)
    coef_a, coef_b = coef_of(alpha)
    side = stencil(station - i, coef_a, coef_b)
    below = jnp.where(i == 0, 0.0, alpha)
    above = jnp.where(i == n - 1, 0.0, alpha)
    return reduce_cyclic(below, jnp.ones_like(alpha), above, [side], 0, (1, 2, 4, 8, 16, 32))[0]


def y_local(alpha_row, gy):
    alpha = jnp.broadcast_to(column(alpha_row, CY, lambda i: i + gy * CY), (CY, 128))
    i = iota((CY, 128), 0)
    c = iota((CY, 128), 1)
    coef_a, coef_b = coef_of(alpha)
    own = stencil(c % CY - i, coef_a, coef_b)
    term = (c - FIELDS * CY) // FIELDS
    at = jnp.where(term == 0, 0, jnp.where(term == 1, 1, jnp.where(term == 2, CY - 1, CY - 2)))
    unit = jnp.where(at == i, 1.0, 0.0)
    side = jnp.where(c < FIELDS * CY, own, jnp.where(c < FIELDS * (CY + 4), unit, 0.0))
    below = jnp.where(i == 0, 0.0, alpha)
    above = jnp.where(i == CY - 1, 0.0, alpha)
    return reduce_cyclic(below, jnp.ones_like(alpha), above, [side], 0, (1, 2, 4, 8))[0]


def y_summary(local):
    r = iota((YROWS, 128), 0)
    c = iota((YROWS, 128), 1)
    value = r // FIELDS
    j = c % CY
    first = jnp.broadcast_to(local[0:1], (YROWS, 128))
    last = jnp.broadcast_to(local[CY - 1 : CY], (YROWS, 128))
    at = jnp.where(value == 2, 0, jnp.where(value == 3, 1, jnp.where(value == 4, CY - 2, CY - 1)))
    out = jnp.where(value == 0, first, jnp.where(value == 1, last, jnp.where(at == j, 1.0, 0.0)))
    keep = (r % FIELDS == c // CY) & (c < FIELDS * CY) & (r < 6 * FIELDS)
    return jnp.where(keep, out, 0.0)


def y_final(local, metric):
    scaled = local * metric
    tall = jnp.concatenate([scaled] * FIELDS, axis=0)
    f = iota(tall.shape, 0) // CY
    c = iota(tall.shape, 1)
    inner = jnp.where(c < FIELDS * CY, c // CY, (c - FIELDS * CY) % FIELDS)
    keep = (f == inner) & (c < FIELDS * (CY + 4))
    return jnp.where(keep, tall, 0.0)


def y_owner_coefs(alpha_row, store):
    shape = (NGY, 128)
    width = alpha_row.shape[1]
    wide = jnp.broadcast_to(alpha_row, (NGY, width))
    lanes = iota((NGY, width), 1)
    masked = jnp.where(lanes // CY == iota((NGY, width), 0), wide, 0.0)
    fold = jnp.where(iota((width, 128), 0) % CY == iota((width, 128), 1), 1.0, 0.0)
    alpha = jnp.dot(masked, fold, precision=HIGH, preferred_element_type=F32)
    b = iota(shape, 0)
    j = iota(shape, 1)
    below = jnp.where((j == 0) | (j >= CY), 0.0, alpha)
    above = jnp.where(j >= CY - 1, 0.0, alpha)
    sides = [jnp.where(j == at, 1.0, 0.0) for at in (0, 1, CY - 1, CY - 2)]
    solved = reduce_cyclic(below, jnp.ones(shape, F32), above, sides, 1, (1, 2, 4, 8))

    def pick(array, lane):
        one = jnp.sum(jnp.where(j == lane, array, 0.0), axis=1, keepdims=True)
        return jnp.broadcast_to(one, shape)

    first = [pick(s, 0) for s in solved]
    last = [pick(s, CY - 1) for s in solved]
    a0, a1 = pick(alpha, 0), pick(alpha, 1)
    ae, af = pick(alpha, CY - 2), pick(alpha, CY - 1)
    low = jnp.where(b == 0, 0.0, a0)
    high = jnp.where(b == NGY - 1, 0.0, af)
    ca0, cb0 = coef_of(a0)
    cb1 = coef_of(a1)[1]
    cbe = coef_of(ae)[1]
    caf, cbf = coef_of(af)
    has_left = b > 0
    has_right = b < NGY - 1
    store(0, jnp.where(has_left, -0.5 * ca0, 0.0))
    store(1, jnp.where(has_left, -0.25 * cb0, 0.0))
    store(2, jnp.where(has_left, -0.25 * cb1, 0.0))
    store(3, jnp.where(has_right, 0.5 * caf, 0.0))
    store(4, jnp.where(has_right, 0.25 * cbf, 0.0))
    store(5, jnp.where(has_right, 0.25 * cbe, 0.0))
    for k in range(4):
        store(6 + k, first[k])
        store(10 + k, last[k])
    store(14, low)
    store(15, high)
    k00, kf0 = low * first[0], low * last[0]
    k0f, kff = high * first[2], high * last[2]
    ratio = jnp.zeros((1, 128), F32)
    invs, ts, ratios = [], [], []
    for block in range(NGY):
        row = slice(block, block + 1)
        inv = 1.0 / (1.0 + k00[row] * ratio)
        t = kf0[row] * ratio * inv
        ratio = t * k0f[row] - kff[row]
        invs.append(inv)
        ts.append(t)
        ratios.append(ratio)
    inv = jnp.concatenate(invs, axis=0)
    t = jnp.concatenate(ts, axis=0)
    store(16, t)
    store(17, t * k00 - kf0)
    store(18, inv)
    store(19, inv * k00)
    store(20, inv * k0f)
    store(21, jnp.concatenate(ratios, axis=0))


def body(
    adj_h, jx_h, jy_h, ax_ref, mx_ref, ay_ref, my_ref, sv_ref, sc_ref, so_ref,
    out_ref,
    adj, jx, jy, fx, fy, xs, xr, xm, xres, xs2, xr2, ysend, yrecv, ycoef, yback, yret,
    sa_send, sa_recv, sa_sum, sb_send, sb_recv, dx,
    in_sem, x1s, x1r, x2s, x2r, y1s, y1r, y2s, y2r, sas, sar, sbs, sbr,
):
    gx = lax.axis_index("gx")
    gy = lax.axis_index("gy")

    loads = [
        pltpu.make_async_copy(adj_h, adj, in_sem.at[0]),
        pltpu.make_async_copy(jx_h, jx, in_sem.at[1]),
        pltpu.make_async_copy(jy_h, jy, in_sem.at[2]),
    ]
    for load in loads:
        load.start()

    barrier = pltpu.get_barrier_semaphore()

    def greet(d, carry):
        pl.semaphore_signal(barrier, inc=1, device_id=(lax.rem(gx + d, NGX), gy), device_id_type=MESH)
        pl.semaphore_signal(barrier, inc=1, device_id=(gx, lax.rem(gy + d, NGY)), device_id_type=MESH)
        return carry

    lax.fori_loop(1, 16, greet, 0)

    def rows(ref, index, count):
        return ref.at[pl.ds(pl.multiple_of(index * count, 8), count)]

    def along_x(src, dst, count, ssem, rsem, d):
        peer = lax.rem(gx + d, NGX)
        return pltpu.make_async_remote_copy(
            src_ref=rows(src, peer, count),
            dst_ref=rows(dst, gx, count),
            send_sem=ssem.at[peer],
            recv_sem=rsem.at[gx],
            device_id=(peer, gy),
            device_id_type=MESH,
        )

    def wait_along_x(src, dst, count, ssem, rsem, d):
        peer = lax.rem(gx + d, NGX)
        copy = pltpu.make_async_remote_copy(
            src_ref=rows(src, peer, count),
            dst_ref=rows(dst, peer, count),
            send_sem=ssem.at[peer],
            recv_sem=rsem.at[peer],
            device_id=(peer, gy),
            device_id_type=MESH,
        )
        copy.wait_recv()
        return copy

    def along_y(src, dst, count, ssem, rsem, d):
        peer = lax.rem(gy + d, NGY)
        return pltpu.make_async_remote_copy(
            src_ref=rows(src, peer, count),
            dst_ref=rows(dst, gy, count),
            send_sem=ssem.at[peer],
            recv_sem=rsem.at[gy],
            device_id=(gx, peer),
            device_id_type=MESH,
        )

    def arriving_along_y(src, dst, count, ssem, rsem, d):
        peer = lax.rem(gy + d, NGY)
        return pltpu.make_async_remote_copy(
            src_ref=rows(src, peer, count),
            dst_ref=rows(dst, peer, count),
            send_sem=ssem.at[peer],
            recv_sem=rsem.at[peer],
            device_id=(gx, peer),
            device_id_type=MESH,
        )

    def each(fn):
        def step(d, carry):
            fn(d)
            return carry

        lax.fori_loop(1, 16, step, 0)

    loads[0].wait()
    loads[1].wait()

    def flux(jac, s, f):
        total = jac[0, f, s].astype(F32) * adj[0, s]
        for k in range(1, FIELDS):
            total = total + jac[k, f, s].astype(F32) * adj[k, s]
        return total

    for s in range(CX):
        for f in range(FIELDS):
            plane = flux(jx, s, f)
            at = (f * CX + s) * CY
            fx[0, at : at + CY] = plane[:, :128]
            fx[1, at : at + CY] = plane[:, 128:]
    for k in range(NGX):
        for half in range(2):
            at = k * XROWS + half * 20
            xs[at : at + 20] = fx[half, pl.ds(k, 20, stride=CY)]
    xr[pl.ds(pl.multiple_of(gx * XROWS, 8), XROWS)] = xs[pl.ds(pl.multiple_of(gx * XROWS, 8), XROWS)]

    pl.semaphore_wait(barrier, 30)
    each(lambda d: along_x(xs, xr, XROWS, x1s, x1r, d).start())

    loads[2].wait()
    for s in range(CX):
        for f in range(FIELDS):
            fy[s, f * CY : (f + 1) * CY] = flux(jy, s, f)
    local = y_local(ay_ref[...], gy)
    summary = y_summary(local)[:, : FIELDS * CY]
    for s in range(CX):
        values = jnp.dot(summary, fy[s], precision=HIGH, preferred_element_type=F32)
        ysend[s * YROWS : (s + 1) * YROWS] = values[:, :128]
        ysend[(CX + s) * YROWS : (CX + s + 1) * YROWS] = values[:, 128:]

    is_owner = lax.rem(gy, 2) == 0
    my_owner = gy // 2

    def to_owner(o):
        return pltpu.make_async_remote_copy(
            src_ref=rows(ysend, o, YROWS),
            dst_ref=rows(yrecv, gy, YROWS),
            send_sem=y1s.at[o],
            recv_sem=y1r.at[gy],
            device_id=(gx, 2 * o),
            device_id_type=MESH,
        )

    def from_block(b):
        return pltpu.make_async_remote_copy(
            src_ref=rows(ysend, my_owner, YROWS),
            dst_ref=rows(yrecv, b, YROWS),
            send_sem=y1s.at[my_owner],
            recv_sem=y1r.at[b],
            device_id=(gx, b),
            device_id_type=MESH,
        )

    def to_block(b):
        return pltpu.make_async_remote_copy(
            src_ref=rows(yback, b, RROWS),
            dst_ref=rows(yret, my_owner, RROWS),
            send_sem=y2s.at[b],
            recv_sem=y2r.at[my_owner],
            device_id=(gx, b),
            device_id_type=MESH,
        )

    def from_owner(o):
        return pltpu.make_async_remote_copy(
            src_ref=rows(yback, 0, RROWS),
            dst_ref=rows(yret, o, RROWS),
            send_sem=y2s.at[0],
            recv_sem=y2r.at[o],
            device_id=(gx, 2 * o),
            device_id_type=MESH,
        )

    def each_owner(fn):
        def step(o, carry):
            @pl.when(2 * o != gy)
            def _():
                fn(o)

            return carry

        lax.fori_loop(0, OWNERS, step, 0)

    each_owner(lambda o: to_owner(o).start())

    @pl.when(is_owner)
    def _():
        yrecv[pl.ds(pl.multiple_of(gy * YROWS, 8), YROWS)] = ysend[
            pl.ds(pl.multiple_of(my_owner * YROWS, 8), YROWS)
        ]

    owner_row = so_ref[...].astype(F32)
    owner_col = jnp.transpose(jnp.broadcast_to(owner_row, (128, POINTS)))
    ranks = []
    for q in range(POINTS // 128):
        mine = owner_row[:, q * 128 : (q + 1) * 128]
        reach = (q + 1) * 128
        same = owner_col[:reach] == jnp.broadcast_to(mine, (reach, 128))
        before = iota((reach, 128), 0) < iota((reach, 128), 1) + q * 128
        ranks.append(jnp.sum(jnp.where(same & before, 1.0, 0.0), axis=0, keepdims=True))
    rank_row = jnp.concatenate(ranks, axis=1)
    r32 = iota((32, POINTS), 0)
    packed = jnp.zeros((32, POINTS), F32)
    for v in range(FIELDS):
        packed = jnp.where(r32 // 4 == v, jnp.broadcast_to(sv_ref[v : v + 1], (32, POINTS)), packed)
    cells = sc_ref[...].astype(F32)
    packed = jnp.where(r32 // 4 == FIELDS, jnp.broadcast_to(cells, (32, POINTS)), packed)
    slot = (r32 % 4).astype(F32) == jnp.broadcast_to(rank_row, (32, POINTS))
    packed = jnp.where(slot & (r32 < 24), packed, 0.0)
    tall = jnp.concatenate([packed] * 4, axis=0)
    tall = jnp.where(iota(tall.shape, 0) // 32 == lax.rem(gx, 4), tall, 0.0)
    part0 = tall.astype(BF16)
    rest = tall - part0.astype(F32)
    part1 = rest.astype(BF16)
    part2 = (rest - part1.astype(F32)).astype(BF16)
    hot = iota((NGX * NGY, POINTS), 0).astype(F32) == jnp.broadcast_to(owner_row, (NGX * NGY, POINTS))
    hot = jnp.where(hot, 1.0, 0.0).astype(BF16)

    def by_lanes(a, b):
        return lax.dot_general(a, b, (((1,), (1,)), ((), ())), preferred_element_type=F32)

    sa_send[...] = by_lanes(hot, part0) + by_lanes(hot, part1) + by_lanes(hot, part2)
    sa_recv[pl.ds(pl.multiple_of(gx * NGY, 8), NGY)] = sa_send[pl.ds(pl.multiple_of(gx * NGY, 8), NGY)]
    each(lambda d: along_x(sa_send, sa_recv, NGY, sas, sar, d).start())

    xm[...] = x_matrix(ax_ref[...])

    @pl.when(is_owner)
    def _():
        def store(k, value):
            ycoef[k] = value

        y_owner_coefs(ay_ref[...], store)

    final = y_final(local, jnp.broadcast_to(column(my_ref[...], CY, lambda i: i), (CY, 128)))

    each(lambda d: wait_along_x(xs, xr, XROWS, x1s, x1r, d) and None)
    matrix = jnp.concatenate([xm[pl.ds(s, NGX, stride=CX)] for s in range(CX)], axis=0)[:, : NGX * CX]
    for g in range(2 * FIELDS):
        lines = jnp.concatenate(
            [xr[pl.ds(g * CX + s, NGX, stride=XROWS)] for s in range(CX)], axis=0
        )
        xres[g * 64 : (g + 1) * 64] = jnp.dot(matrix, lines, precision=HIGH, preferred_element_type=F32)
    for k in range(NGX):
        xs2[k * XROWS : (k + 1) * XROWS] = xres[pl.ds(k, XROWS, stride=NGX)]
    xr2[pl.ds(pl.multiple_of(gx * XROWS, 8), XROWS)] = xs2[pl.ds(pl.multiple_of(gx * XROWS, 8), XROWS)]
    each(lambda d: along_x(xs2, xr2, XROWS, x2s, x2r, d).start())

    @pl.when(is_owner)
    def _():
        def arrive(b, carry):
            @pl.when(b != gy)
            def _():
                from_block(b).wait_recv()

            return carry

        lax.fori_loop(0, NGY, arrive, 0)
        shape = (FIELDS, 128)

        def get(b, v):
            at = b * YROWS + v * FIELDS
            return yrecv[at : at + FIELDS]

        def coef(k, b):
            return jnp.broadcast_to(ycoef[k, b : b + 1], shape)

        firsts, lasts, c_part, d_part, c1s, d1s = [], [], [], [], [], []
        for b in range(NGY):
            p, q = get(b, 0), get(b, 1)
            zero = jnp.zeros(shape, F32)
            c0 = c1 = d0 = d1 = zero
            if b > 0:
                left1, left2 = get(b - 1, 5), get(b - 1, 4)
                c0 = coef(0, b) * left1 + coef(1, b) * left2
                c1 = coef(2, b) * left1
                p = p + coef(6, b) * c0 + coef(7, b) * c1
                q = q + coef(10, b) * c0 + coef(11, b) * c1
            if b < NGY - 1:
                right1, right2 = get(b + 1, 2), get(b + 1, 3)
                d0 = coef(3, b) * right1 + coef(4, b) * right2
                d1 = coef(5, b) * right1
                p = p + coef(8, b) * d0 + coef(9, b) * d1
                q = q + coef(12, b) * d0 + coef(13, b) * d1
            firsts.append(p)
            lasts.append(q)
            c_part.append(c0)
            c1s.append(c1)
            d_part.append(d0)
            d1s.append(d1)
        entering = [jnp.zeros(shape, F32)]
        for b in range(NGY):
            entering.append(
                lasts[b] - coef(16, b) * firsts[b] + coef(17, b) * entering[b]
            )
        heads = [None] * NGY + [jnp.zeros(shape, F32)]
        for b in range(NGY - 1, -1, -1):
            heads[b] = (
                coef(18, b) * firsts[b] - coef(19, b) * entering[b] - coef(20, b) * heads[b + 1]
            )
        pad = jnp.zeros((RROWS - 4 * FIELDS, 128), F32)
        for b in range(NGY):
            c0, d0 = c_part[b], d_part[b]
            if b > 0:
                left = entering[b] + coef(21, b - 1) * heads[b]
                c0 = c0 - coef(14, b) * left
            if b < NGY - 1:
                d0 = d0 - coef(15, b) * heads[b + 1]
            at = b * RROWS
            yback[at : at + RROWS] = jnp.concatenate([c0, c1s[b], d0, d1s[b], pad], axis=0)
        yret[pl.ds(pl.multiple_of(my_owner * RROWS, 8), RROWS)] = yback[
            pl.ds(pl.multiple_of(gy * RROWS, 8), RROWS)
        ]

        def reply(b, carry):
            @pl.when(b != gy)
            def _():
                to_block(b).start()

            return carry

        lax.fori_loop(0, NGY, reply, 0)

    each(lambda d: wait_along_x(sa_send, sa_recv, NGY, sas, sar, d) and None)
    for g in range(4):
        at = g * 4 * NGY
        sa_sum[g * NGY : (g + 1) * NGY] = (
            sa_recv[at : at + NGY]
            + sa_recv[at + NGY : at + 2 * NGY]
            + sa_recv[at + 2 * NGY : at + 3 * NGY]
            + sa_recv[at + 3 * NGY : at + 4 * NGY]
        )
    odd = jnp.broadcast_to(lax.rem(gy, 2) == 1, (8, 128))
    upper = iota((8, 128), 0) >= 4
    for k in range(NGY):
        piece = sa_sum[pl.ds(k, 4, stride=NGY)]
        both = jnp.concatenate([piece, piece], axis=0)
        sb_send[k * 8 : (k + 1) * 8] = jnp.where(upper == odd, both, 0.0)
    sb_recv[pl.ds(pl.multiple_of(gy * 8, 8), 8)] = sb_send[pl.ds(pl.multiple_of(gy * 8, 8), 8)]
    each(lambda d: along_y(sb_send, sb_recv, 8, sbs, sbr, d).start())
    each(lambda d: arriving_along_y(sb_send, sb_recv, 8, sbs, sbr, d).wait_recv())

    data = jnp.concatenate(
        [sb_recv[16 * j : 16 * j + 8] + sb_recv[16 * j + 8 : 16 * j + 16] for j in range(8)], axis=0
    )
    pairs = jnp.concatenate([data, pltpu.roll(data, 96, 1)], axis=0)
    turned = jnp.transpose(pairs)
    turned_hi = turned.astype(BF16).astype(F32)
    turned_lo = turned - turned_hi
    row_ids = iota((64, 128), 0)
    depth_ids = iota((128, CZ), 1)
    lefts, rights = [], []
    for h in range(2):
        for s in range(4):
            at = 64 * h + 4 * FIELDS + s
            cell = turned[at : at + 1].astype(jnp.int32)
            here = jnp.broadcast_to(cell // CZ, (64, 128)) == row_ids
            for source in (turned_hi, turned_lo):
                tall = [
                    jnp.where(
                        here,
                        jnp.broadcast_to(
                            source[64 * h + 4 * f + s : 64 * h + 4 * f + s + 1], (64, 128)
                        ),
                        0.0,
                    )
                    for f in range(FIELDS)
                ]
                lefts.append(jnp.concatenate(tall, axis=0).astype(BF16))
            cell_col = pairs[:, at : at + 1].astype(jnp.int32) % CZ
            deep = jnp.broadcast_to(cell_col, (128, CZ)) == depth_ids
            deep = jnp.where(deep, 1.0, 0.0).astype(BF16)
            rights.append(deep)
            rights.append(deep)
    forcing = jnp.zeros((FIELDS * CX * CY, CZ), F32)
    for left, right in zip(lefts, rights):
        forcing = forcing + jnp.dot(left, right, preferred_element_type=F32)

    each_owner(lambda o: from_owner(o).wait_recv())
    metric_rows = column(mx_ref[...], 20, lambda i: lax.rem(i, CX))
    deriv_y = []
    for s in range(CX):
        reply = jnp.concatenate(
            [yret[s * RROWS : (s + 1) * RROWS], yret[(CX + s) * RROWS : (CX + s + 1) * RROWS]], axis=1
        )
        known = jnp.concatenate([fy[s], reply], axis=0)
        deriv_y.append(
            jnp.dot(
                final[:, : FIELDS * CY + RROWS], known, precision=HIGH, preferred_element_type=F32
            )
        )

    each(lambda d: wait_along_x(xs2, xr2, XROWS, x2s, x2r, d) and None)
    for k in range(NGX):
        for half in range(2):
            at = k * XROWS + half * 20
            dx[half, pl.ds(k, 20, stride=CY)] = xr2[at : at + 20] * metric_rows
    for f in range(FIELDS):
        for s in range(CX):
            at = (f * CX + s) * CY
            along = jnp.concatenate([dx[0, at : at + CY], dx[1, at : at + CY]], axis=1)
            out_ref[f, s] = forcing[at : at + CY] - (along + deriv_y[s][f * CY : (f + 1) * CY])

    each(lambda d: along_x(xs, xr, XROWS, x1s, x1r, d).wait_send())
    each(lambda d: along_x(sa_send, sa_recv, NGY, sas, sar, d).wait_send())
    each(lambda d: along_x(xs2, xr2, XROWS, x2s, x2r, d).wait_send())
    each(lambda d: along_y(sb_send, sb_recv, 8, sbs, sbr, d).wait_send())
    each_owner(lambda o: to_owner(o).wait_send())

    @pl.when(is_owner)
    def _():
        def sent(b, carry):
            @pl.when(b != gy)
            def _():
                to_block(b).wait_send()

            return carry

        lax.fori_loop(0, NGY, sent, 0)


def on_device(
    adjoint, jac_x, jac_y, alpha_x, metric_x, alpha_y, metric_y, surf_values, surf_cells, surf_owner
):
    vmem = pl.BlockSpec(memory_space=pltpu.VMEM)
    anywhere = pl.BlockSpec(memory_space=pl.ANY)
    dma = pltpu.SemaphoreType.DMA((16,))
    return pl.pallas_call(
        body,
        out_shape=jax.ShapeDtypeStruct((FIELDS, CX, CY, CZ), F32),
        in_specs=[anywhere] * 3 + [vmem] * 7,
        out_specs=vmem,
        scratch_shapes=[
            pltpu.VMEM((FIELDS, CX, CY, CZ), F32),
            pltpu.VMEM((FIELDS, FIELDS, CX, CY, CZ), BF16),
            pltpu.VMEM((FIELDS, FIELDS, CX, CY, CZ), BF16),
            pltpu.VMEM((2, FIELDS * CX * CY, 128), F32),
            pltpu.VMEM((CX, FIELDS * CY, CZ), F32),
            pltpu.VMEM((NGX * XROWS, 128), F32),
            pltpu.VMEM((NGX * XROWS, 128), F32),
            pltpu.VMEM((NGX * CX, 128), F32),
            pltpu.VMEM((2 * FIELDS * NGX * CX, 128), F32),
            pltpu.VMEM((NGX * XROWS, 128), F32),
            pltpu.VMEM((NGX * XROWS, 128), F32),
            pltpu.VMEM((OWNERS * YROWS, 128), F32),
            pltpu.VMEM((NGY * YROWS, 128), F32),
            pltpu.VMEM((22, NGY, 128), F32),
            pltpu.VMEM((NGY * RROWS, 128), F32),
            pltpu.VMEM((OWNERS * RROWS, 128), F32),
            pltpu.VMEM((NGX * NGY, 128), F32),
            pltpu.VMEM((NGX * NGY, 128), F32),
            pltpu.VMEM((4 * NGY, 128), F32),
            pltpu.VMEM((NGY * 8, 128), F32),
            pltpu.VMEM((NGY * 8, 128), F32),
            pltpu.VMEM((2, FIELDS * CX * CY, 128), F32),
            pltpu.SemaphoreType.DMA((3,)),
        ]
        + [dma] * 12,
        compiler_params=pltpu.CompilerParams(
            collective_id=0, has_side_effects=True, vmem_limit_bytes=48 * 1024 * 1024
        ),
    )(
        adjoint,
        jac_x,
        jac_y,
        alpha_x.reshape(1, -1),
        metric_x.reshape(1, -1),
        alpha_y.reshape(1, -1),
        metric_y.reshape(1, -1),
        surf_values.reshape(FIELDS, POINTS),
        surf_cells.reshape(1, POINTS),
        surf_owner.reshape(1, POINTS),
    )


def solution(mesh):
    in_specs = (
        P(None, "gx", "gy", None),
        P(None, None, "gx", "gy", None),
        P(None, None, "gx", "gy", None),
        P(),
        P("gx"),
        P(),
        P("gy"),
        P(("gx", "gy"), None, None),
        P(("gx", "gy"), None),
        P(("gx", "gy"), None, None),
    )
    return jax.shard_map(
        on_device,
        mesh=mesh,
        in_specs=in_specs,
        out_specs=P(None, "gx", "gy", None),
        check_vma=False,
    )
```

```python
import functools

import jax
import jax.numpy as jnp
from jax import lax
from jax.experimental import pallas as pl
from jax.experimental.pallas import tpu as pltpu
from jax.sharding import PartitionSpec as P

F32 = jnp.float32
BF16 = jnp.bfloat16
MESH = pl.DeviceIdType.MESH
FIELDS = 5
CX = 4
CY = 16
CZ = 256
NGX = 16
NGY = 16
POINTS = 512
OWNERS = 8
XROWS = 40
YROWS = 32
SROWS = 8
RROWS = 24
FULL = lax.Precision.HIGHEST
HIGH = lax.Precision.HIGH
FAR_FIRST = (8, 7, 9, 6, 10, 5, 11, 4, 12, 3, 13, 2, 14, 1, 15)


def iota(shape, dim):
    return lax.broadcasted_iota(jnp.int32, shape, dim)


def column(row, rows, lane_of):
    width = row.shape[1]
    wide = jnp.broadcast_to(row, (rows, width))
    picked = iota((rows, width), 1) == lane_of(iota((rows, width), 0))
    return jnp.sum(jnp.where(picked, wide, 0.0), axis=1, keepdims=True)


def reduce_cyclic(below, diag, above, sides, axis, distances):
    count = below.shape[axis]
    for d in distances:
        inv = 1.0 / diag
        low = -below * pltpu.roll(inv, d, axis)
        high = -above * pltpu.roll(inv, count - d, axis)
        sides = [
            s + low * pltpu.roll(s, d, axis) + high * pltpu.roll(s, count - d, axis) for s in sides
        ]
        diag = diag + low * pltpu.roll(above, d, axis) + high * pltpu.roll(below, count - d, axis)
        below = low * pltpu.roll(below, d, axis)
        above = high * pltpu.roll(above, count - d, axis)
    inv = 1.0 / diag
    return [s * inv for s in sides]


def stencil(offset, coef_a, coef_b):
    zero = jnp.zeros_like(coef_a)
    out = jnp.where(offset == 1, 0.5 * coef_a, zero)
    out = jnp.where(offset == -1, -0.5 * coef_a, out)
    out = jnp.where(offset == 2, 0.25 * coef_b, out)
    return jnp.where(offset == -2, -0.25 * coef_b, out)


def coef_of(alpha):
    return (2.0 / 3.0) * (alpha + 2.0), (4.0 * alpha - 1.0) / 3.0


def x_matrix(alpha_row):
    n = NGX * CX
    alpha = jnp.broadcast_to(column(alpha_row, n, lambda i: i), (n, 128))
    i = iota((n, 128), 0)
    c = iota((n, 128), 1)
    station = jnp.where(c < n, (c % NGX) * CX + c // NGX, -100)
    coef_a, coef_b = coef_of(alpha)
    side = stencil(station - i, coef_a, coef_b)
    below = jnp.where(i == 0, 0.0, alpha)
    above = jnp.where(i == n - 1, 0.0, alpha)
    return reduce_cyclic(below, jnp.ones_like(alpha), above, [side], 0, (1, 2, 4, 8, 16, 32))[0]


def y_local(alpha_row, gy):
    alpha = jnp.broadcast_to(column(alpha_row, CY, lambda i: i + gy * CY), (CY, 128))
    i = iota((CY, 128), 0)
    c = iota((CY, 128), 1)
    coef_a, coef_b = coef_of(alpha)
    own = stencil(c % CY - i, coef_a, coef_b)
    term = (c - FIELDS * CY) // FIELDS
    at = jnp.where(term == 0, 0, jnp.where(term == 1, 1, jnp.where(term == 2, CY - 1, CY - 2)))
    unit = jnp.where(at == i, 1.0, 0.0)
    side = jnp.where(c < FIELDS * CY, own, jnp.where(c < FIELDS * (CY + 4), unit, 0.0))
    below = jnp.where(i == 0, 0.0, alpha)
    above = jnp.where(i == CY - 1, 0.0, alpha)
    return reduce_cyclic(below, jnp.ones_like(alpha), above, [side], 0, (1, 2, 4, 8))[0]


def y_summary(local):
    r = iota((YROWS, 128), 0)
    c = iota((YROWS, 128), 1)
    value = r // FIELDS
    j = c % CY
    first = jnp.broadcast_to(local[0:1], (YROWS, 128))
    last = jnp.broadcast_to(local[CY - 1 : CY], (YROWS, 128))
    at = jnp.where(value == 2, 0, jnp.where(value == 3, 1, jnp.where(value == 4, CY - 2, CY - 1)))
    out = jnp.where(value == 0, first, jnp.where(value == 1, last, jnp.where(at == j, 1.0, 0.0)))
    keep = (r % FIELDS == c // CY) & (c < FIELDS * CY) & (r < 6 * FIELDS)
    return jnp.where(keep, out, 0.0)


def y_final(local, metric):
    scaled = local * metric
    tall = jnp.concatenate([scaled] * FIELDS, axis=0)
    f = iota(tall.shape, 0) // CY
    c = iota(tall.shape, 1)
    inner = jnp.where(c < FIELDS * CY, c // CY, (c - FIELDS * CY) % FIELDS)
    keep = (f == inner) & (c < FIELDS * (CY + 4))
    return jnp.where(keep, tall, 0.0)


def y_owner_coefs(alpha_row, store):
    shape = (NGY, 128)
    width = alpha_row.shape[1]
    wide = jnp.broadcast_to(alpha_row, (NGY, width))
    lanes = iota((NGY, width), 1)
    masked = jnp.where(lanes // CY == iota((NGY, width), 0), wide, 0.0)
    fold = jnp.where(iota((width, 128), 0) % CY == iota((width, 128), 1), 1.0, 0.0)
    alpha = jnp.dot(masked, fold, precision=FULL, preferred_element_type=F32)
    b = iota(shape, 0)
    j = iota(shape, 1)
    below = jnp.where((j == 0) | (j >= CY), 0.0, alpha)
    above = jnp.where(j >= CY - 1, 0.0, alpha)
    sides = [jnp.where(j == at, 1.0, 0.0) for at in (0, 1, CY - 1, CY - 2)]
    solved = reduce_cyclic(below, jnp.ones(shape, F32), above, sides, 1, (1, 2, 4, 8))

    def pick(array, lane):
        one = jnp.sum(jnp.where(j == lane, array, 0.0), axis=1, keepdims=True)
        return jnp.broadcast_to(one, shape)

    first = [pick(s, 0) for s in solved]
    last = [pick(s, CY - 1) for s in solved]
    a0, a1 = pick(alpha, 0), pick(alpha, 1)
    ae, af = pick(alpha, CY - 2), pick(alpha, CY - 1)
    low = jnp.where(b == 0, 0.0, a0)
    high = jnp.where(b == NGY - 1, 0.0, af)
    ca0, cb0 = coef_of(a0)
    cb1 = coef_of(a1)[1]
    cbe = coef_of(ae)[1]
    caf, cbf = coef_of(af)
    has_left = b > 0
    has_right = b < NGY - 1
    store(0, jnp.where(has_left, -0.5 * ca0, 0.0))
    store(1, jnp.where(has_left, -0.25 * cb0, 0.0))
    store(2, jnp.where(has_left, -0.25 * cb1, 0.0))
    store(3, jnp.where(has_right, 0.5 * caf, 0.0))
    store(4, jnp.where(has_right, 0.25 * cbf, 0.0))
    store(5, jnp.where(has_right, 0.25 * cbe, 0.0))
    for k in range(4):
        store(6 + k, first[k])
        store(10 + k, last[k])
    store(14, low)
    store(15, high)
    k00, kf0 = low * first[0], low * last[0]
    k0f, kff = high * first[2], high * last[2]
    ratio = jnp.zeros((1, 128), F32)
    invs, ts, ratios = [], [], []
    for block in range(NGY):
        row = slice(block, block + 1)
        inv = 1.0 / (1.0 + k00[row] * ratio)
        t = kf0[row] * ratio * inv
        ratio = t * k0f[row] - kff[row]
        invs.append(inv)
        ts.append(t)
        ratios.append(ratio)
    inv = jnp.concatenate(invs, axis=0)
    t = jnp.concatenate(ts, axis=0)
    store(16, t)
    store(17, t * k00 - kf0)
    store(18, inv)
    store(19, inv * k00)
    store(20, inv * k0f)
    store(21, jnp.concatenate(ratios, axis=0))


def body(
    adj_h, jx_h, jy_h, ax_h, mx_h, ay_h, my_h, sv_h, sc_h, so_h,
    out_ref,
    adj, jx, jy, ax_ref, mx_ref, ay_ref, my_ref, sv_ref, sc_ref, so_ref, fx, fy, xs, xr, xm, xres, xs2, xr2, ysend, yrecv, ycoef, yback, yret,
    sa_send, sa_recv, sa_sum, sb_send, sb_recv, dx,
    in_sem, x1s, x1r, x2s, x2r, y1s, y1r, y2s, y2r, sas, sar, sbs, sbr,
):
    gx = lax.axis_index("gx")
    gy = lax.axis_index("gy")

    barrier = pltpu.get_barrier_semaphore()

    def after(position, d):
        ahead = position + d
        return jnp.where(ahead >= 16, ahead - 16, ahead)

    for d in FAR_FIRST:
        pl.semaphore_signal(barrier, inc=1, device_id=(after(gx, d), gy), device_id_type=MESH)
        pl.semaphore_signal(barrier, inc=1, device_id=(gx, after(gy, d)), device_id_type=MESH)

    loads = [
        pltpu.make_async_copy(adj_h, adj, in_sem.at[0]),
        pltpu.make_async_copy(jx_h, jx, in_sem.at[1]),
        pltpu.make_async_copy(jy_h, jy, in_sem.at[2]),
        pltpu.make_async_copy(ay_h, ay_ref, in_sem.at[3]),
        pltpu.make_async_copy(so_h, so_ref, in_sem.at[4]),
        pltpu.make_async_copy(sv_h, sv_ref, in_sem.at[5]),
        pltpu.make_async_copy(sc_h, sc_ref, in_sem.at[6]),
        pltpu.make_async_copy(ax_h, ax_ref, in_sem.at[7]),
        pltpu.make_async_copy(mx_h, mx_ref, in_sem.at[8]),
        pltpu.make_async_copy(my_h, my_ref, in_sem.at[9]),
    ]
    for load in loads:
        load.start()

    def rows(ref, index, count):
        return ref.at[pl.ds(pl.multiple_of(index * count, 8), count)]

    def along_x(src, dst, count, ssem, rsem, d):
        peer = after(gx, d)
        return pltpu.make_async_remote_copy(
            src_ref=rows(src, peer, count),
            dst_ref=rows(dst, gx, count),
            send_sem=ssem.at[peer],
            recv_sem=rsem.at[gx],
            device_id=(peer, gy),
            device_id_type=MESH,
        )

    def wait_along_x(src, dst, count, ssem, rsem, d):
        peer = after(gx, d)
        copy = pltpu.make_async_remote_copy(
            src_ref=rows(src, peer, count),
            dst_ref=rows(dst, peer, count),
            send_sem=ssem.at[peer],
            recv_sem=rsem.at[peer],
            device_id=(peer, gy),
            device_id_type=MESH,
        )
        copy.wait_recv()
        return copy

    def along_y(src, dst, count, ssem, rsem, d):
        peer = after(gy, d)
        return pltpu.make_async_remote_copy(
            src_ref=rows(src, peer, count),
            dst_ref=rows(dst, gy, count),
            send_sem=ssem.at[peer],
            recv_sem=rsem.at[gy],
            device_id=(gx, peer),
            device_id_type=MESH,
        )

    def arriving_along_y(src, dst, count, ssem, rsem, d):
        peer = after(gy, d)
        return pltpu.make_async_remote_copy(
            src_ref=rows(src, peer, count),
            dst_ref=rows(dst, peer, count),
            send_sem=ssem.at[peer],
            recv_sem=rsem.at[peer],
            device_id=(gx, peer),
            device_id_type=MESH,
        )

    def each(fn):
        for d in FAR_FIRST:
            fn(d)

    loads[0].wait()
    loads[1].wait()

    def flux(jac, s, f):
        total = jac[0, f, s].astype(F32) * adj[0, s]
        for k in range(1, FIELDS):
            total = total + jac[k, f, s].astype(F32) * adj[k, s]
        return total

    for s in range(CX):
        for f in range(FIELDS):
            plane = flux(jx, s, f)
            at = (f * CX + s) * CY
            fx[0, at : at + CY] = plane[:, :128]
            fx[1, at : at + CY] = plane[:, 128:]
    for k in range(NGX):
        for half in range(2):
            at = k * XROWS + half * 20
            xs[at : at + 20] = fx[half, pl.ds(k, 20, stride=CY)]
    xr[pl.ds(pl.multiple_of(gx * XROWS, 8), XROWS)] = xs[pl.ds(pl.multiple_of(gx * XROWS, 8), XROWS)]

    for load in loads[2:]:
        load.wait()
    for s in range(CX):
        for f in range(FIELDS):
            fy[s, f * CY : (f + 1) * CY] = flux(jy, s, f)
    local = y_local(ay_ref[...], gy)
    summary = y_summary(local)[:, : FIELDS * CY]
    for s in range(CX):
        values = jnp.dot(summary, fy[s], precision=FULL, preferred_element_type=F32)
        ysend[s * YROWS : (s + 1) * YROWS] = values[:, :128]
        ysend[(CX + s) * YROWS : (CX + s + 1) * YROWS] = values[:, 128:]

    is_owner = lax.rem(gy, 2) == 0
    my_owner = gy // 2

    def to_owner(o):
        return pltpu.make_async_remote_copy(
            src_ref=rows(ysend, o, YROWS),
            dst_ref=rows(yrecv, gy, YROWS),
            send_sem=y1s.at[o],
            recv_sem=y1r.at[gy],
            device_id=(gx, 2 * o),
            device_id_type=MESH,
        )

    def from_block(b):
        return pltpu.make_async_remote_copy(
            src_ref=rows(ysend, my_owner, YROWS),
            dst_ref=rows(yrecv, b, YROWS),
            send_sem=y1s.at[my_owner],
            recv_sem=y1r.at[b],
            device_id=(gx, b),
            device_id_type=MESH,
        )

    def to_block(b):
        return pltpu.make_async_remote_copy(
            src_ref=rows(yback, b, RROWS),
            dst_ref=rows(yret, my_owner, RROWS),
            send_sem=y2s.at[b],
            recv_sem=y2r.at[my_owner],
            device_id=(gx, b),
            device_id_type=MESH,
        )

    def from_owner(o):
        return pltpu.make_async_remote_copy(
            src_ref=rows(yback, 0, RROWS),
            dst_ref=rows(yret, o, RROWS),
            send_sem=y2s.at[0],
            recv_sem=y2r.at[o],
            device_id=(gx, 2 * o),
            device_id_type=MESH,
        )

    def each_owner(fn):
        for o in range(OWNERS):

            @pl.when(2 * o != gy)
            def _():
                fn(o)

    @pl.when(is_owner)
    def _():
        yrecv[pl.ds(pl.multiple_of(gy * YROWS, 8), YROWS)] = ysend[
            pl.ds(pl.multiple_of(my_owner * YROWS, 8), YROWS)
        ]

    owner_row = so_ref[...].astype(F32)
    owner_col = jnp.transpose(jnp.broadcast_to(owner_row, (128, POINTS)))
    ranks = []
    for q in range(POINTS // 128):
        mine = owner_row[:, q * 128 : (q + 1) * 128]
        reach = (q + 1) * 128
        same = owner_col[:reach] == jnp.broadcast_to(mine, (reach, 128))
        before = iota((reach, 128), 0) < iota((reach, 128), 1) + q * 128
        ranks.append(jnp.sum(jnp.where(same & before, 1.0, 0.0), axis=0, keepdims=True))
    rank_row = jnp.concatenate(ranks, axis=1)
    r32 = iota((32, POINTS), 0)
    packed = jnp.zeros((32, POINTS), F32)
    for v in range(FIELDS):
        packed = jnp.where(r32 // 4 == v, jnp.broadcast_to(sv_ref[v], (32, POINTS)), packed)
    cells = sc_ref[...].astype(F32)
    packed = jnp.where(r32 // 4 == FIELDS, jnp.broadcast_to(cells, (32, POINTS)), packed)
    slot = (r32 % 4).astype(F32) == jnp.broadcast_to(rank_row, (32, POINTS))
    packed = jnp.where(slot & (r32 < 24), packed, 0.0)
    owner_int = so_ref[...]
    block = (owner_int + gx) % 4
    tall = jnp.concatenate([packed] * 4, axis=0)
    tall = jnp.where(iota(tall.shape, 0) // 32 == jnp.broadcast_to(block, tall.shape), tall, 0.0)
    part0 = tall.astype(BF16)
    rest = tall - part0.astype(F32)
    part1 = rest.astype(BF16)
    part2 = (rest - part1.astype(F32)).astype(BF16)
    place = owner_int // NGY * SROWS + owner_int % NGY // 4
    hot = iota((NGX * SROWS, POINTS), 0) == jnp.broadcast_to(place, (NGX * SROWS, POINTS))
    hot = jnp.where(hot, 1.0, 0.0).astype(BF16)

    def by_lanes(a, b):
        return lax.dot_general(a, b, (((1,), (1,)), ((), ())), preferred_element_type=F32)

    sa_send[...] = by_lanes(hot, part0) + by_lanes(hot, part1) + by_lanes(hot, part2)
    sa_recv[pl.ds(pl.multiple_of(gx * SROWS, 8), SROWS)] = sa_send[
        pl.ds(pl.multiple_of(gx * SROWS, 8), SROWS)
    ]

    pl.semaphore_wait(barrier, 30)
    each_owner(lambda o: to_owner(o).start())
    each(lambda d: along_x(sa_send, sa_recv, SROWS, sas, sar, d).start())
    each(lambda d: along_x(xs, xr, XROWS, x1s, x1r, d).start())

    xm[...] = x_matrix(ax_ref[...])

    @pl.when(is_owner)
    def _():
        def store(k, value):
            ycoef[k] = value

        y_owner_coefs(ay_ref[...], store)

    final = y_final(local, jnp.broadcast_to(column(my_ref[...], CY, lambda i: i), (CY, 128)))

    each(lambda d: wait_along_x(sa_send, sa_recv, SROWS, sas, sar, d) and None)
    sources = [
        jnp.concatenate(
            [sa_recv[(4 * g + q) * SROWS : (4 * g + q + 1) * SROWS] for g in range(4)], axis=0
        )
        for q in range(4)
    ]
    lane_block = iota((4 * SROWS, 128), 1) // 32
    for g in range(4):
        merged = sources[0]
        for q in range(1, 4):
            merged = jnp.where(lane_block == (g + q) % 4, sources[q], merged)
        sa_sum[g * 4 * SROWS : (g + 1) * 4 * SROWS] = merged
    odd = jnp.broadcast_to(lax.rem(gy, 2) == 1, (8, 128))
    upper = iota((8, 128), 0) >= 4
    for k in range(NGY):
        piece = sa_sum[pl.ds(k % 4 * 4 * SROWS + k // 4, 4, stride=SROWS)]
        both = jnp.concatenate([piece, piece], axis=0)
        sb_send[k * 8 : (k + 1) * 8] = jnp.where(upper == odd, both, 0.0)
    sb_recv[pl.ds(pl.multiple_of(gy * 8, 8), 8)] = sb_send[pl.ds(pl.multiple_of(gy * 8, 8), 8)]
    each(lambda d: along_y(sb_send, sb_recv, 8, sbs, sbr, d).start())

    each(lambda d: wait_along_x(xs, xr, XROWS, x1s, x1r, d) and None)
    matrix = jnp.concatenate([xm[pl.ds(s, NGX, stride=CX)] for s in range(CX)], axis=0)[:, : NGX * CX]
    for g in range(2 * FIELDS):
        lines = jnp.concatenate(
            [xr[pl.ds(g * CX + s, NGX, stride=XROWS)] for s in range(CX)], axis=0
        )
        xres[g * 64 : (g + 1) * 64] = jnp.dot(matrix, lines, precision=HIGH, preferred_element_type=F32)
    for k in range(NGX):
        xs2[k * XROWS : (k + 1) * XROWS] = xres[pl.ds(k, XROWS, stride=NGX)]
    xr2[pl.ds(pl.multiple_of(gx * XROWS, 8), XROWS)] = xs2[pl.ds(pl.multiple_of(gx * XROWS, 8), XROWS)]
    each(lambda d: along_x(xs2, xr2, XROWS, x2s, x2r, d).start())

    @pl.when(is_owner)
    def _():
        def arrive(b, carry):
            @pl.when(b != gy)
            def _():
                from_block(b).wait_recv()

            return carry

        lax.fori_loop(0, NGY, arrive, 0)
        shape = (FIELDS, 128)

        def get(b, v):
            at = b * YROWS + v * FIELDS
            return yrecv[at : at + FIELDS]

        def coef(k, b):
            return jnp.broadcast_to(ycoef[k, b : b + 1], shape)

        firsts, lasts, c_part, d_part, c1s, d1s = [], [], [], [], [], []
        for b in range(NGY):
            p, q = get(b, 0), get(b, 1)
            zero = jnp.zeros(shape, F32)
            c0 = c1 = d0 = d1 = zero
            if b > 0:
                left1, left2 = get(b - 1, 5), get(b - 1, 4)
                c0 = coef(0, b) * left1 + coef(1, b) * left2
                c1 = coef(2, b) * left1
                p = p + coef(6, b) * c0 + coef(7, b) * c1
                q = q + coef(10, b) * c0 + coef(11, b) * c1
            if b < NGY - 1:
                right1, right2 = get(b + 1, 2), get(b + 1, 3)
                d0 = coef(3, b) * right1 + coef(4, b) * right2
                d1 = coef(5, b) * right1
                p = p + coef(8, b) * d0 + coef(9, b) * d1
                q = q + coef(12, b) * d0 + coef(13, b) * d1
            firsts.append(p)
            lasts.append(q)
            c_part.append(c0)
            c1s.append(c1)
            d_part.append(d0)
            d1s.append(d1)
        entering = [jnp.zeros(shape, F32)]
        for b in range(NGY):
            entering.append(
                lasts[b] - coef(16, b) * firsts[b] + coef(17, b) * entering[b]
            )
        heads = [None] * NGY + [jnp.zeros(shape, F32)]
        for b in range(NGY - 1, -1, -1):
            heads[b] = (
                coef(18, b) * firsts[b] - coef(19, b) * entering[b] - coef(20, b) * heads[b + 1]
            )
        pad = jnp.zeros((RROWS - 4 * FIELDS, 128), F32)
        for b in range(NGY):
            c0, d0 = c_part[b], d_part[b]
            if b > 0:
                left = entering[b] + coef(21, b - 1) * heads[b]
                c0 = c0 - coef(14, b) * left
            if b < NGY - 1:
                d0 = d0 - coef(15, b) * heads[b + 1]
            at = b * RROWS
            yback[at : at + RROWS] = jnp.concatenate([c0, c1s[b], d0, d1s[b], pad], axis=0)
        yret[pl.ds(pl.multiple_of(my_owner * RROWS, 8), RROWS)] = yback[
            pl.ds(pl.multiple_of(gy * RROWS, 8), RROWS)
        ]

        def reply(b, carry):
            @pl.when(b != gy)
            def _():
                to_block(b).start()

            return carry

        lax.fori_loop(0, NGY, reply, 0)

    each(lambda d: arriving_along_y(sb_send, sb_recv, 8, sbs, sbr, d).wait_recv())

    data = jnp.concatenate(
        [sb_recv[16 * j : 16 * j + 8] + sb_recv[16 * j + 8 : 16 * j + 16] for j in range(8)], axis=0
    )
    pairs = jnp.concatenate([data, pltpu.roll(data, 96, 1)], axis=0)
    turned = jnp.transpose(pairs)
    turned_hi = turned.astype(BF16).astype(F32)
    turned_lo = turned - turned_hi
    row_ids = iota((64, 128), 0)
    depth_ids = iota((128, CZ), 1)
    lefts, rights = [], []
    for h in range(2):
        for s in range(4):
            at = 64 * h + 4 * FIELDS + s
            cell = turned[at : at + 1].astype(jnp.int32)
            here = jnp.broadcast_to(cell // CZ, (64, 128)) == row_ids
            for source in (turned_hi, turned_lo):
                tall = [
                    jnp.where(
                        here,
                        jnp.broadcast_to(
                            source[64 * h + 4 * f + s : 64 * h + 4 * f + s + 1], (64, 128)
                        ),
                        0.0,
                    )
                    for f in range(FIELDS)
                ]
                lefts.append(jnp.concatenate(tall, axis=0).astype(BF16))
            cell_col = pairs[:, at : at + 1].astype(jnp.int32) % CZ
            deep = jnp.broadcast_to(cell_col, (128, CZ)) == depth_ids
            deep = jnp.where(deep, 1.0, 0.0).astype(BF16)
            rights.append(deep)
            rights.append(deep)
    forcing = jnp.zeros((FIELDS * CX * CY, CZ), F32)
    for left, right in zip(lefts, rights):
        forcing = forcing + jnp.dot(left, right, preferred_element_type=F32)

    metric_rows = column(mx_ref[...], 20, lambda i: lax.rem(i, CX))
    known = [
        jnp.dot(final[:, : FIELDS * CY], fy[s], precision=HIGH, preferred_element_type=F32)
        for s in range(CX)
    ]
    for f in range(FIELDS):
        for s in range(CX):
            at = (f * CX + s) * CY
            out_ref[f, s] = forcing[at : at + CY] - known[s][f * CY : (f + 1) * CY]

    each(lambda d: along_x(xs, xr, XROWS, x1s, x1r, d).wait_send())
    each(lambda d: along_x(sa_send, sa_recv, SROWS, sas, sar, d).wait_send())
    each(lambda d: along_y(sb_send, sb_recv, 8, sbs, sbr, d).wait_send())
    each_owner(lambda o: to_owner(o).wait_send())

    each(lambda d: wait_along_x(xs2, xr2, XROWS, x2s, x2r, d) and None)
    for k in range(NGX):
        for half in range(2):
            at = k * XROWS + half * 20
            dx[half, pl.ds(k, 20, stride=CY)] = xr2[at : at + 20] * metric_rows
    for f in range(FIELDS):
        for s in range(CX):
            at = (f * CX + s) * CY
            along = jnp.concatenate([dx[0, at : at + CY], dx[1, at : at + CY]], axis=1)
            out_ref[f, s] = out_ref[f, s] - along
    each(lambda d: along_x(xs2, xr2, XROWS, x2s, x2r, d).wait_send())

    @pl.when(is_owner)
    def _():
        for b in range(NGY):

            @pl.when(b != gy)
            def _():
                to_block(b).wait_send()

    each_owner(lambda o: from_owner(o).wait_recv())
    for s in range(CX):
        reply = jnp.concatenate(
            [yret[s * RROWS : (s + 1) * RROWS], yret[(CX + s) * RROWS : (CX + s + 1) * RROWS]], axis=1
        )
        extra = jnp.dot(
            final[:, FIELDS * CY : FIELDS * CY + RROWS],
            reply,
            precision=HIGH,
            preferred_element_type=F32,
        )
        for f in range(FIELDS):
            out_ref[f, s] = out_ref[f, s] - extra[f * CY : (f + 1) * CY]


def on_device(
    adjoint, jac_x, jac_y, alpha_x, metric_x, alpha_y, metric_y, surf_values, surf_cells, surf_owner
):
    vmem = pl.BlockSpec(memory_space=pltpu.VMEM)
    hbm = pl.BlockSpec(memory_space=pltpu.HBM)
    dma = pltpu.SemaphoreType.DMA((16,))
    return pl.pallas_call(
        body,
        out_shape=jax.ShapeDtypeStruct((FIELDS, CX, CY, CZ), F32),
        in_specs=[hbm] * 10,
        out_specs=vmem,
        scratch_shapes=[
            pltpu.VMEM((FIELDS, CX, CY, CZ), F32),
            pltpu.VMEM((FIELDS, FIELDS, CX, CY, CZ), BF16),
            pltpu.VMEM((FIELDS, FIELDS, CX, CY, CZ), BF16),
            pltpu.VMEM((1, NGX * CX), F32),
            pltpu.VMEM((1, CX), F32),
            pltpu.VMEM((1, NGY * CY), F32),
            pltpu.VMEM((1, CY), F32),
            pltpu.VMEM((FIELDS, 1, POINTS), F32),
            pltpu.VMEM((1, POINTS), jnp.int32),
            pltpu.VMEM((1, POINTS), jnp.int32),
            pltpu.VMEM((2, FIELDS * CX * CY, 128), F32),
            pltpu.VMEM((CX, FIELDS * CY, CZ), F32),
            pltpu.VMEM((NGX * XROWS, 128), F32),
            pltpu.VMEM((NGX * XROWS, 128), F32),
            pltpu.VMEM((NGX * CX, 128), F32),
            pltpu.VMEM((2 * FIELDS * NGX * CX, 128), F32),
            pltpu.VMEM((NGX * XROWS, 128), F32),
            pltpu.VMEM((NGX * XROWS, 128), F32),
            pltpu.VMEM((OWNERS * YROWS, 128), F32),
            pltpu.VMEM((NGY * YROWS, 128), F32),
            pltpu.VMEM((22, NGY, 128), F32),
            pltpu.VMEM((NGY * RROWS, 128), F32),
            pltpu.VMEM((OWNERS * RROWS, 128), F32),
            pltpu.VMEM((NGX * SROWS, 128), F32),
            pltpu.VMEM((NGX * SROWS, 128), F32),
            pltpu.VMEM((16 * SROWS, 128), F32),
            pltpu.VMEM((NGY * 8, 128), F32),
            pltpu.VMEM((NGY * 8, 128), F32),
            pltpu.VMEM((2, FIELDS * CX * CY, 128), F32),
            pltpu.SemaphoreType.DMA((10,)),
        ]
        + [dma] * 12,
        compiler_params=pltpu.CompilerParams(
            collective_id=0, has_side_effects=True, vmem_limit_bytes=67043328
        ),
    )(
        adjoint,
        jac_x,
        jac_y,
        alpha_x.reshape(1, -1),
        metric_x.reshape(1, -1),
        alpha_y.reshape(1, -1),
        metric_y.reshape(1, -1),
        surf_values.reshape(FIELDS, 1, POINTS),
        surf_cells.reshape(1, POINTS),
        surf_owner.reshape(1, POINTS),
    )


def solution(mesh):
    in_specs = (
        P(None, "gx", "gy", None),
        P(None, None, "gx", "gy", None),
        P(None, None, "gx", "gy", None),
        P(),
        P("gx"),
        P(),
        P("gy"),
        P(("gx", "gy"), None, None),
        P(("gx", "gy"), None),
        P(("gx", "gy"), None, None),
    )
    return jax.shard_map(
        on_device,
        mesh=mesh,
        in_specs=in_specs,
        out_specs=P(None, "gx", "gy", None),
        check_vma=False,
    )
```

```python
import functools

import jax
import jax.numpy as jnp
from jax import lax
from jax.experimental import pallas as pl
from jax.experimental.pallas import tpu as pltpu
from jax.sharding import PartitionSpec as P

F32 = jnp.float32
BF16 = jnp.bfloat16
MESH = pl.DeviceIdType.MESH
FIELDS = 5
CX = 4
CY = 16
CZ = 256
NGX = 16
NGY = 16
POINTS = 512
OWNERS = 8
XROWS = 40
YROWS = 32
SROWS = 8
RROWS = 24
FULL = lax.Precision.HIGHEST
HIGH = lax.Precision.HIGH
FAR_FIRST = tuple(range(1, 16))


def iota(shape, dim):
    return lax.broadcasted_iota(jnp.int32, shape, dim)


def column(row, rows, lane_of):
    width = row.shape[1]
    wide = jnp.broadcast_to(row, (rows, width))
    picked = iota((rows, width), 1) == lane_of(iota((rows, width), 0))
    return jnp.sum(jnp.where(picked, wide, 0.0), axis=1, keepdims=True)


def reduce_cyclic(below, diag, above, sides, axis, distances):
    count = below.shape[axis]
    for d in distances:
        inv = 1.0 / diag
        low = -below * pltpu.roll(inv, d, axis)
        high = -above * pltpu.roll(inv, count - d, axis)
        sides = [
            s + low * pltpu.roll(s, d, axis) + high * pltpu.roll(s, count - d, axis) for s in sides
        ]
        diag = diag + low * pltpu.roll(above, d, axis) + high * pltpu.roll(below, count - d, axis)
        below = low * pltpu.roll(below, d, axis)
        above = high * pltpu.roll(above, count - d, axis)
    inv = 1.0 / diag
    return [s * inv for s in sides]


def stencil(offset, coef_a, coef_b):
    zero = jnp.zeros_like(coef_a)
    out = jnp.where(offset == 1, 0.5 * coef_a, zero)
    out = jnp.where(offset == -1, -0.5 * coef_a, out)
    out = jnp.where(offset == 2, 0.25 * coef_b, out)
    return jnp.where(offset == -2, -0.25 * coef_b, out)


def coef_of(alpha):
    return (2.0 / 3.0) * (alpha + 2.0), (4.0 * alpha - 1.0) / 3.0


def x_matrix(alpha_row):
    n = NGX * CX
    alpha = jnp.broadcast_to(column(alpha_row, n, lambda i: i), (n, 128))
    i = iota((n, 128), 0)
    c = iota((n, 128), 1)
    station = jnp.where(c < n, (c % NGX) * CX + c // NGX, -100)
    coef_a, coef_b = coef_of(alpha)
    side = stencil(station - i, coef_a, coef_b)
    below = jnp.where(i == 0, 0.0, alpha)
    above = jnp.where(i == n - 1, 0.0, alpha)
    return reduce_cyclic(below, jnp.ones_like(alpha), above, [side], 0, (1, 2, 4, 8, 16, 32))[0]


def y_local(alpha_row, gy):
    alpha = jnp.broadcast_to(column(alpha_row, CY, lambda i: i + gy * CY), (CY, 128))
    i = iota((CY, 128), 0)
    c = iota((CY, 128), 1)
    coef_a, coef_b = coef_of(alpha)
    own = stencil(c % CY - i, coef_a, coef_b)
    term = (c - FIELDS * CY) // FIELDS
    at = jnp.where(term == 0, 0, jnp.where(term == 1, 1, jnp.where(term == 2, CY - 1, CY - 2)))
    unit = jnp.where(at == i, 1.0, 0.0)
    side = jnp.where(c < FIELDS * CY, own, jnp.where(c < FIELDS * (CY + 4), unit, 0.0))
    below = jnp.where(i == 0, 0.0, alpha)
    above = jnp.where(i == CY - 1, 0.0, alpha)
    return reduce_cyclic(below, jnp.ones_like(alpha), above, [side], 0, (1, 2, 4, 8))[0]


def y_summary(local):
    r = iota((YROWS, 128), 0)
    c = iota((YROWS, 128), 1)
    value = r // FIELDS
    j = c % CY
    first = jnp.broadcast_to(local[0:1], (YROWS, 128))
    last = jnp.broadcast_to(local[CY - 1 : CY], (YROWS, 128))
    at = jnp.where(value == 2, 0, jnp.where(value == 3, 1, jnp.where(value == 4, CY - 2, CY - 1)))
    out = jnp.where(value == 0, first, jnp.where(value == 1, last, jnp.where(at == j, 1.0, 0.0)))
    keep = (r % FIELDS == c // CY) & (c < FIELDS * CY) & (r < 6 * FIELDS)
    return jnp.where(keep, out, 0.0)


def y_final(local, metric):
    scaled = local * metric
    tall = jnp.concatenate([scaled] * FIELDS, axis=0)
    f = iota(tall.shape, 0) // CY
    c = iota(tall.shape, 1)
    inner = jnp.where(c < FIELDS * CY, c // CY, (c - FIELDS * CY) % FIELDS)
    keep = (f == inner) & (c < FIELDS * (CY + 4))
    return jnp.where(keep, tall, 0.0)


def y_owner_coefs(alpha_row, store):
    shape = (NGY, 128)
    width = alpha_row.shape[1]
    wide = jnp.broadcast_to(alpha_row, (NGY, width))
    lanes = iota((NGY, width), 1)
    masked = jnp.where(lanes // CY == iota((NGY, width), 0), wide, 0.0)
    fold = jnp.where(iota((width, 128), 0) % CY == iota((width, 128), 1), 1.0, 0.0)
    alpha = jnp.dot(masked, fold, precision=FULL, preferred_element_type=F32)
    b = iota(shape, 0)
    j = iota(shape, 1)
    below = jnp.where((j == 0) | (j >= CY), 0.0, alpha)
    above = jnp.where(j >= CY - 1, 0.0, alpha)
    sides = [jnp.where(j == at, 1.0, 0.0) for at in (0, 1, CY - 1, CY - 2)]
    solved = reduce_cyclic(below, jnp.ones(shape, F32), above, sides, 1, (1, 2, 4, 8))

    def pick(array, lane):
        one = jnp.sum(jnp.where(j == lane, array, 0.0), axis=1, keepdims=True)
        return jnp.broadcast_to(one, shape)

    first = [pick(s, 0) for s in solved]
    last = [pick(s, CY - 1) for s in solved]
    a0, a1 = pick(alpha, 0), pick(alpha, 1)
    ae, af = pick(alpha, CY - 2), pick(alpha, CY - 1)
    low = jnp.where(b == 0, 0.0, a0)
    high = jnp.where(b == NGY - 1, 0.0, af)
    ca0, cb0 = coef_of(a0)
    cb1 = coef_of(a1)[1]
    cbe = coef_of(ae)[1]
    caf, cbf = coef_of(af)
    has_left = b > 0
    has_right = b < NGY - 1
    store(0, jnp.where(has_left, -0.5 * ca0, 0.0))
    store(1, jnp.where(has_left, -0.25 * cb0, 0.0))
    store(2, jnp.where(has_left, -0.25 * cb1, 0.0))
    store(3, jnp.where(has_right, 0.5 * caf, 0.0))
    store(4, jnp.where(has_right, 0.25 * cbf, 0.0))
    store(5, jnp.where(has_right, 0.25 * cbe, 0.0))
    for k in range(4):
        store(6 + k, first[k])
        store(10 + k, last[k])
    store(14, low)
    store(15, high)
    k00, kf0 = low * first[0], low * last[0]
    k0f, kff = high * first[2], high * last[2]
    ratio = jnp.zeros((1, 128), F32)
    invs, ts, ratios = [], [], []
    for block in range(NGY):
        row = slice(block, block + 1)
        inv = 1.0 / (1.0 + k00[row] * ratio)
        t = kf0[row] * ratio * inv
        ratio = t * k0f[row] - kff[row]
        invs.append(inv)
        ts.append(t)
        ratios.append(ratio)
    inv = jnp.concatenate(invs, axis=0)
    t = jnp.concatenate(ts, axis=0)
    store(16, t)
    store(17, t * k00 - kf0)
    store(18, inv)
    store(19, inv * k00)
    store(20, inv * k0f)
    store(21, jnp.concatenate(ratios, axis=0))


def body(
    adj_h, jx_h, jy_h, ax_h, mx_h, ay_h, my_h, sv_h, sc_h, so_h,
    out_ref,
    adj, jx, jy, ax_ref, mx_ref, ay_ref, my_ref, sv_ref, sc_ref, so_ref, fx, fy, xs, xr, xm, xres, xs2, xr2, ysend, yrecv, ycoef, yback, yret,
    sa_send, sa_recv, sa_sum, sb_send, sb_recv, dx,
    in_sem, x1s, x1r, x2s, x2r, y1s, y1r, y2s, y2r, sas, sar, sbs, sbr,
):
    gx = lax.axis_index("gx")
    gy = lax.axis_index("gy")

    barrier = pltpu.get_barrier_semaphore()

    def after(position, d):
        ahead = position + d
        return jnp.where(ahead >= 16, ahead - 16, ahead)

    for d in FAR_FIRST:
        pl.semaphore_signal(barrier, inc=1, device_id=(after(gx, d), gy), device_id_type=MESH)
        pl.semaphore_signal(barrier, inc=1, device_id=(gx, after(gy, d)), device_id_type=MESH)

    loads = [
        pltpu.make_async_copy(adj_h, adj, in_sem.at[0]),
        pltpu.make_async_copy(jx_h, jx, in_sem.at[1]),
        pltpu.make_async_copy(jy_h, jy, in_sem.at[2]),
        pltpu.make_async_copy(ay_h, ay_ref, in_sem.at[3]),
        pltpu.make_async_copy(so_h, so_ref, in_sem.at[4]),
        pltpu.make_async_copy(sv_h, sv_ref, in_sem.at[5]),
        pltpu.make_async_copy(sc_h, sc_ref, in_sem.at[6]),
        pltpu.make_async_copy(ax_h, ax_ref, in_sem.at[7]),
        pltpu.make_async_copy(mx_h, mx_ref, in_sem.at[8]),
        pltpu.make_async_copy(my_h, my_ref, in_sem.at[9]),
    ]
    for load in loads:
        load.start()

    def rows(ref, index, count):
        return ref.at[pl.ds(pl.multiple_of(index * count, 8), count)]

    def along_x(src, dst, count, ssem, rsem, d):
        peer = after(gx, d)
        return pltpu.make_async_remote_copy(
            src_ref=rows(src, peer, count),
            dst_ref=rows(dst, gx, count),
            send_sem=ssem.at[peer],
            recv_sem=rsem.at[gx],
            device_id=(peer, gy),
            device_id_type=MESH,
        )

    def wait_along_x(src, dst, count, ssem, rsem, d):
        peer = after(gx, d)
        copy = pltpu.make_async_remote_copy(
            src_ref=rows(src, peer, count),
            dst_ref=rows(dst, peer, count),
            send_sem=ssem.at[peer],
            recv_sem=rsem.at[peer],
            device_id=(peer, gy),
            device_id_type=MESH,
        )
        copy.wait_recv()
        return copy

    def along_y(src, dst, count, ssem, rsem, d):
        peer = after(gy, d)
        return pltpu.make_async_remote_copy(
            src_ref=rows(src, peer, count),
            dst_ref=rows(dst, gy, count),
            send_sem=ssem.at[peer],
            recv_sem=rsem.at[gy],
            device_id=(gx, peer),
            device_id_type=MESH,
        )

    def arriving_along_y(src, dst, count, ssem, rsem, d):
        peer = after(gy, d)
        return pltpu.make_async_remote_copy(
            src_ref=rows(src, peer, count),
            dst_ref=rows(dst, peer, count),
            send_sem=ssem.at[peer],
            recv_sem=rsem.at[peer],
            device_id=(gx, peer),
            device_id_type=MESH,
        )

    def each(fn):
        for d in FAR_FIRST:
            fn(d)

    loads[0].wait()
    loads[1].wait()

    def flux(jac, s, f):
        total = jac[0, f, s].astype(F32) * adj[0, s]
        for k in range(1, FIELDS):
            total = total + jac[k, f, s].astype(F32) * adj[k, s]
        return total

    for s in range(CX):
        for f in range(FIELDS):
            plane = flux(jx, s, f)
            at = (f * CX + s) * CY
            fx[0, at : at + CY] = plane[:, :128]
            fx[1, at : at + CY] = plane[:, 128:]
    for k in range(NGX):
        for half in range(2):
            at = k * XROWS + half * 20
            xs[at : at + 20] = fx[half, pl.ds(k, 20, stride=CY)]
    xr[pl.ds(pl.multiple_of(gx * XROWS, 8), XROWS)] = xs[pl.ds(pl.multiple_of(gx * XROWS, 8), XROWS)]

    for load in loads[2:]:
        load.wait()
    for s in range(CX):
        for f in range(FIELDS):
            fy[s, f * CY : (f + 1) * CY] = flux(jy, s, f)
    local = y_local(ay_ref[...], gy)
    summary = y_summary(local)[:, : FIELDS * CY]
    for s in range(CX):
        values = jnp.dot(summary, fy[s], precision=FULL, preferred_element_type=F32)
        ysend[s * YROWS : (s + 1) * YROWS] = values[:, :128]
        ysend[(CX + s) * YROWS : (CX + s + 1) * YROWS] = values[:, 128:]

    is_owner = lax.rem(gy, 2) == 0
    my_owner = gy // 2

    def to_owner(o):
        return pltpu.make_async_remote_copy(
            src_ref=rows(ysend, o, YROWS),
            dst_ref=rows(yrecv, gy, YROWS),
            send_sem=y1s.at[o],
            recv_sem=y1r.at[gy],
            device_id=(gx, 2 * o),
            device_id_type=MESH,
        )

    def from_block(b):
        return pltpu.make_async_remote_copy(
            src_ref=rows(ysend, my_owner, YROWS),
            dst_ref=rows(yrecv, b, YROWS),
            send_sem=y1s.at[my_owner],
            recv_sem=y1r.at[b],
            device_id=(gx, b),
            device_id_type=MESH,
        )

    def to_block(b):
        return pltpu.make_async_remote_copy(
            src_ref=rows(yback, b, RROWS),
            dst_ref=rows(yret, my_owner, RROWS),
            send_sem=y2s.at[b],
            recv_sem=y2r.at[my_owner],
            device_id=(gx, b),
            device_id_type=MESH,
        )

    def from_owner(o):
        return pltpu.make_async_remote_copy(
            src_ref=rows(yback, 0, RROWS),
            dst_ref=rows(yret, o, RROWS),
            send_sem=y2s.at[0],
            recv_sem=y2r.at[o],
            device_id=(gx, 2 * o),
            device_id_type=MESH,
        )

    def each_owner(fn):
        for o in range(OWNERS):

            @pl.when(2 * o != gy)
            def _():
                fn(o)

    @pl.when(is_owner)
    def _():
        yrecv[pl.ds(pl.multiple_of(gy * YROWS, 8), YROWS)] = ysend[
            pl.ds(pl.multiple_of(my_owner * YROWS, 8), YROWS)
        ]

    owner_row = so_ref[...].astype(F32)
    owner_col = jnp.transpose(jnp.broadcast_to(owner_row, (128, POINTS)))
    ranks = []
    for q in range(POINTS // 128):
        mine = owner_row[:, q * 128 : (q + 1) * 128]
        reach = (q + 1) * 128
        same = owner_col[:reach] == jnp.broadcast_to(mine, (reach, 128))
        before = iota((reach, 128), 0) < iota((reach, 128), 1) + q * 128
        ranks.append(jnp.sum(jnp.where(same & before, 1.0, 0.0), axis=0, keepdims=True))
    rank_row = jnp.concatenate(ranks, axis=1)
    r32 = iota((32, POINTS), 0)
    packed = jnp.zeros((32, POINTS), F32)
    for v in range(FIELDS):
        packed = jnp.where(r32 // 4 == v, jnp.broadcast_to(sv_ref[v], (32, POINTS)), packed)
    cells = sc_ref[...].astype(F32)
    packed = jnp.where(r32 // 4 == FIELDS, jnp.broadcast_to(cells, (32, POINTS)), packed)
    slot = (r32 % 4).astype(F32) == jnp.broadcast_to(rank_row, (32, POINTS))
    packed = jnp.where(slot & (r32 < 24), packed, 0.0)
    owner_int = so_ref[...]
    block = (owner_int + gx) % 4
    tall = jnp.concatenate([packed] * 4, axis=0)
    tall = jnp.where(iota(tall.shape, 0) // 32 == jnp.broadcast_to(block, tall.shape), tall, 0.0)
    part0 = tall.astype(BF16)
    rest = tall - part0.astype(F32)
    part1 = rest.astype(BF16)
    part2 = (rest - part1.astype(F32)).astype(BF16)
    place = owner_int // NGY * SROWS + owner_int % NGY // 4
    hot = iota((NGX * SROWS, POINTS), 0) == jnp.broadcast_to(place, (NGX * SROWS, POINTS))
    hot = jnp.where(hot, 1.0, 0.0).astype(BF16)

    def by_lanes(a, b):
        return lax.dot_general(a, b, (((1,), (1,)), ((), ())), preferred_element_type=F32)

    sa_send[...] = by_lanes(hot, part0) + by_lanes(hot, part1) + by_lanes(hot, part2)
    sa_recv[pl.ds(pl.multiple_of(gx * SROWS, 8), SROWS)] = sa_send[
        pl.ds(pl.multiple_of(gx * SROWS, 8), SROWS)
    ]

    pl.semaphore_wait(barrier, 30)
    each_owner(lambda o: to_owner(o).start())
    each(lambda d: along_x(sa_send, sa_recv, SROWS, sas, sar, d).start())
    each(lambda d: along_x(xs, xr, XROWS, x1s, x1r, d).start())

    xm[...] = x_matrix(ax_ref[...])

    @pl.when(is_owner)
    def _():
        def store(k, value):
            ycoef[k] = value

        y_owner_coefs(ay_ref[...], store)

    final = y_final(local, jnp.broadcast_to(column(my_ref[...], CY, lambda i: i), (CY, 128)))

    each(lambda d: wait_along_x(sa_send, sa_recv, SROWS, sas, sar, d) and None)
    sources = [
        jnp.concatenate(
            [sa_recv[(4 * g + q) * SROWS : (4 * g + q + 1) * SROWS] for g in range(4)], axis=0
        )
        for q in range(4)
    ]
    lane_block = iota((4 * SROWS, 128), 1) // 32
    for g in range(4):
        merged = sources[0]
        for q in range(1, 4):
            merged = jnp.where(lane_block == (g + q) % 4, sources[q], merged)
        sa_sum[g * 4 * SROWS : (g + 1) * 4 * SROWS] = merged
    odd = jnp.broadcast_to(lax.rem(gy, 2) == 1, (8, 128))
    upper = iota((8, 128), 0) >= 4
    for k in range(NGY):
        piece = sa_sum[pl.ds(k % 4 * 4 * SROWS + k // 4, 4, stride=SROWS)]
        both = jnp.concatenate([piece, piece], axis=0)
        sb_send[k * 8 : (k + 1) * 8] = jnp.where(upper == odd, both, 0.0)
    sb_recv[pl.ds(pl.multiple_of(gy * 8, 8), 8)] = sb_send[pl.ds(pl.multiple_of(gy * 8, 8), 8)]
    each(lambda d: along_y(sb_send, sb_recv, 8, sbs, sbr, d).start())

    each(lambda d: wait_along_x(xs, xr, XROWS, x1s, x1r, d) and None)
    matrix = jnp.concatenate([xm[pl.ds(s, NGX, stride=CX)] for s in range(CX)], axis=0)[:, : NGX * CX]
    for g in range(2 * FIELDS):
        lines = jnp.concatenate(
            [xr[pl.ds(g * CX + s, NGX, stride=XROWS)] for s in range(CX)], axis=0
        )
        xres[g * 64 : (g + 1) * 64] = jnp.dot(matrix, lines, precision=HIGH, preferred_element_type=F32)
    for k in range(NGX):
        xs2[k * XROWS : (k + 1) * XROWS] = xres[pl.ds(k, XROWS, stride=NGX)]
    xr2[pl.ds(pl.multiple_of(gx * XROWS, 8), XROWS)] = xs2[pl.ds(pl.multiple_of(gx * XROWS, 8), XROWS)]
    each(lambda d: along_x(xs2, xr2, XROWS, x2s, x2r, d).start())

    @pl.when(is_owner)
    def _():
        def arrive(b, carry):
            @pl.when(b != gy)
            def _():
                from_block(b).wait_recv()

            return carry

        lax.fori_loop(0, NGY, arrive, 0)
        shape = (FIELDS, 128)

        def get(b, v):
            at = b * YROWS + v * FIELDS
            return yrecv[at : at + FIELDS]

        def coef(k, b):
            return jnp.broadcast_to(ycoef[k, b : b + 1], shape)

        firsts, lasts, c_part, d_part, c1s, d1s = [], [], [], [], [], []
        for b in range(NGY):
            p, q = get(b, 0), get(b, 1)
            zero = jnp.zeros(shape, F32)
            c0 = c1 = d0 = d1 = zero
            if b > 0:
                left1, left2 = get(b - 1, 5), get(b - 1, 4)
                c0 = coef(0, b) * left1 + coef(1, b) * left2
                c1 = coef(2, b) * left1
                p = p + coef(6, b) * c0 + coef(7, b) * c1
                q = q + coef(10, b) * c0 + coef(11, b) * c1
            if b < NGY - 1:
                right1, right2 = get(b + 1, 2), get(b + 1, 3)
                d0 = coef(3, b) * right1 + coef(4, b) * right2
                d1 = coef(5, b) * right1
                p = p + coef(8, b) * d0 + coef(9, b) * d1
                q = q + coef(12, b) * d0 + coef(13, b) * d1
            firsts.append(p)
            lasts.append(q)
            c_part.append(c0)
            c1s.append(c1)
            d_part.append(d0)
            d1s.append(d1)
        entering = [jnp.zeros(shape, F32)]
        for b in range(NGY):
            entering.append(
                lasts[b] - coef(16, b) * firsts[b] + coef(17, b) * entering[b]
            )
        heads = [None] * NGY + [jnp.zeros(shape, F32)]
        for b in range(NGY - 1, -1, -1):
            heads[b] = (
                coef(18, b) * firsts[b] - coef(19, b) * entering[b] - coef(20, b) * heads[b + 1]
            )
        pad = jnp.zeros((RROWS - 4 * FIELDS, 128), F32)
        for b in range(NGY):
            c0, d0 = c_part[b], d_part[b]
            if b > 0:
                left = entering[b] + coef(21, b - 1) * heads[b]
                c0 = c0 - coef(14, b) * left
            if b < NGY - 1:
                d0 = d0 - coef(15, b) * heads[b + 1]
            at = b * RROWS
            yback[at : at + RROWS] = jnp.concatenate([c0, c1s[b], d0, d1s[b], pad], axis=0)
        yret[pl.ds(pl.multiple_of(my_owner * RROWS, 8), RROWS)] = yback[
            pl.ds(pl.multiple_of(gy * RROWS, 8), RROWS)
        ]

        def reply(b, carry):
            @pl.when(b != gy)
            def _():
                to_block(b).start()

            return carry

        lax.fori_loop(0, NGY, reply, 0)

    each(lambda d: arriving_along_y(sb_send, sb_recv, 8, sbs, sbr, d).wait_recv())

    data = jnp.concatenate(
        [sb_recv[16 * j : 16 * j + 8] + sb_recv[16 * j + 8 : 16 * j + 16] for j in range(8)], axis=0
    )
    pairs = jnp.concatenate([data, pltpu.roll(data, 96, 1)], axis=0)
    turned = jnp.transpose(pairs)
    turned_hi = turned.astype(BF16).astype(F32)
    turned_lo = turned - turned_hi
    row_ids = iota((64, 128), 0)
    depth_ids = iota((128, CZ), 1)
    lefts, rights = [], []
    for h in range(2):
        for s in range(4):
            at = 64 * h + 4 * FIELDS + s
            cell = turned[at : at + 1].astype(jnp.int32)
            here = jnp.broadcast_to(cell // CZ, (64, 128)) == row_ids
            for source in (turned_hi, turned_lo):
                tall = [
                    jnp.where(
                        here,
                        jnp.broadcast_to(
                            source[64 * h + 4 * f + s : 64 * h + 4 * f + s + 1], (64, 128)
                        ),
                        0.0,
                    )
                    for f in range(FIELDS)
                ]
                lefts.append(jnp.concatenate(tall, axis=0).astype(BF16))
            cell_col = pairs[:, at : at + 1].astype(jnp.int32) % CZ
            deep = jnp.broadcast_to(cell_col, (128, CZ)) == depth_ids
            deep = jnp.where(deep, 1.0, 0.0).astype(BF16)
            rights.append(deep)
            rights.append(deep)
    forcing = jnp.zeros((FIELDS * CX * CY, CZ), F32)
    for left, right in zip(lefts, rights):
        forcing = forcing + jnp.dot(left, right, preferred_element_type=F32)

    metric_rows = column(mx_ref[...], 20, lambda i: lax.rem(i, CX))
    known = [
        jnp.dot(final[:, : FIELDS * CY], fy[s], precision=HIGH, preferred_element_type=F32)
        for s in range(CX)
    ]
    for f in range(FIELDS):
        for s in range(CX):
            at = (f * CX + s) * CY
            out_ref[f, s] = forcing[at : at + CY] - known[s][f * CY : (f + 1) * CY]

    each(lambda d: along_x(xs, xr, XROWS, x1s, x1r, d).wait_send())
    each(lambda d: along_x(sa_send, sa_recv, SROWS, sas, sar, d).wait_send())
    each(lambda d: along_y(sb_send, sb_recv, 8, sbs, sbr, d).wait_send())
    each_owner(lambda o: to_owner(o).wait_send())

    each(lambda d: wait_along_x(xs2, xr2, XROWS, x2s, x2r, d) and None)
    for k in range(NGX):
        for half in range(2):
            at = k * XROWS + half * 20
            dx[half, pl.ds(k, 20, stride=CY)] = xr2[at : at + 20] * metric_rows
    for f in range(FIELDS):
        for s in range(CX):
            at = (f * CX + s) * CY
            along = jnp.concatenate([dx[0, at : at + CY], dx[1, at : at + CY]], axis=1)
            out_ref[f, s] = out_ref[f, s] - along
    each(lambda d: along_x(xs2, xr2, XROWS, x2s, x2r, d).wait_send())

    @pl.when(is_owner)
    def _():
        for b in range(NGY):

            @pl.when(b != gy)
            def _():
                to_block(b).wait_send()

    each_owner(lambda o: from_owner(o).wait_recv())
    for s in range(CX):
        reply = jnp.concatenate(
            [yret[s * RROWS : (s + 1) * RROWS], yret[(CX + s) * RROWS : (CX + s + 1) * RROWS]], axis=1
        )
        extra = jnp.dot(
            final[:, FIELDS * CY : FIELDS * CY + RROWS],
            reply,
            precision=HIGH,
            preferred_element_type=F32,
        )
        for f in range(FIELDS):
            out_ref[f, s] = out_ref[f, s] - extra[f * CY : (f + 1) * CY]


def on_device(
    adjoint, jac_x, jac_y, alpha_x, metric_x, alpha_y, metric_y, surf_values, surf_cells, surf_owner
):
    vmem = pl.BlockSpec(memory_space=pltpu.VMEM)
    hbm = pl.BlockSpec(memory_space=pltpu.HBM)
    dma = pltpu.SemaphoreType.DMA((16,))
    pin = lambda a: pltpu.with_memory_space_constraint(a, pltpu.HBM)
    return pl.pallas_call(
        body,
        out_shape=jax.ShapeDtypeStruct((FIELDS, CX, CY, CZ), F32),
        in_specs=[hbm] * 10,
        out_specs=vmem,
        scratch_shapes=[
            pltpu.VMEM((FIELDS, CX, CY, CZ), F32),
            pltpu.VMEM((FIELDS, FIELDS, CX, CY, CZ), BF16),
            pltpu.VMEM((FIELDS, FIELDS, CX, CY, CZ), BF16),
            pltpu.VMEM((1, NGX * CX), F32),
            pltpu.VMEM((1, CX), F32),
            pltpu.VMEM((1, NGY * CY), F32),
            pltpu.VMEM((1, CY), F32),
            pltpu.VMEM((FIELDS, 1, POINTS), F32),
            pltpu.VMEM((1, POINTS), jnp.int32),
            pltpu.VMEM((1, POINTS), jnp.int32),
            pltpu.VMEM((2, FIELDS * CX * CY, 128), F32),
            pltpu.VMEM((CX, FIELDS * CY, CZ), F32),
            pltpu.VMEM((NGX * XROWS, 128), F32),
            pltpu.VMEM((NGX * XROWS, 128), F32),
            pltpu.VMEM((NGX * CX, 128), F32),
            pltpu.VMEM((2 * FIELDS * NGX * CX, 128), F32),
            pltpu.VMEM((NGX * XROWS, 128), F32),
            pltpu.VMEM((NGX * XROWS, 128), F32),
            pltpu.VMEM((OWNERS * YROWS, 128), F32),
            pltpu.VMEM((NGY * YROWS, 128), F32),
            pltpu.VMEM((22, NGY, 128), F32),
            pltpu.VMEM((NGY * RROWS, 128), F32),
            pltpu.VMEM((OWNERS * RROWS, 128), F32),
            pltpu.VMEM((NGX * SROWS, 128), F32),
            pltpu.VMEM((NGX * SROWS, 128), F32),
            pltpu.VMEM((16 * SROWS, 128), F32),
            pltpu.VMEM((NGY * 8, 128), F32),
            pltpu.VMEM((NGY * 8, 128), F32),
            pltpu.VMEM((2, FIELDS * CX * CY, 128), F32),
            pltpu.SemaphoreType.DMA((10,)),
        ]
        + [dma] * 12,
        compiler_params=pltpu.CompilerParams(
            collective_id=0, has_side_effects=True, vmem_limit_bytes=50331648
        ),
    )(
        *map(
            pin,
            (
                adjoint,
                jac_x,
                jac_y,
                alpha_x.reshape(1, -1),
                metric_x.reshape(1, -1),
                alpha_y.reshape(1, -1),
                metric_y.reshape(1, -1),
                surf_values.reshape(FIELDS, 1, POINTS),
                surf_cells.reshape(1, POINTS),
                surf_owner.reshape(1, POINTS),
            ),
        )
    )


def solution(mesh):
    in_specs = (
        P(None, "gx", "gy", None),
        P(None, None, "gx", "gy", None),
        P(None, None, "gx", "gy", None),
        P(),
        P("gx"),
        P(),
        P("gy"),
        P(("gx", "gy"), None, None),
        P(("gx", "gy"), None),
        P(("gx", "gy"), None, None),
    )
    return jax.shard_map(
        on_device,
        mesh=mesh,
        in_specs=in_specs,
        out_specs=P(None, "gx", "gy", None),
        check_vma=False,
    )
```
